256 devices in a mesh: rows: 32 (over z, y), owners: 4 (over x), rep: 2 (over core).
Axes of the slice: x: 4, y: 4, z: 8, core: 2. Of those that a mesh axis runs over, the one named last changes fastest.
Arguments:
- blocks: bfloat16 [6144, 27, 4096], P(('rows', 'owners')), may hold values from -0.75 to 0.75
- panels: bfloat16 [6144, 2, 2048], P(('rows', 'owners'), 'rep'), may hold values from -2 to 2
- columns: int32 [6144, 27], P(('rows', 'owners')), may hold values from 0 to 6143, as said below
- aggregate: int32 [6144], P(('rows', 'owners')), may hold values from 0 to 2047, as said below
- coarse_slots: int32 [6144, 27], P(('rows', 'owners')), may hold values from 0 to 32, as said below
Outputs:
- coarse: float32 [2048, 33, 2, 2048], P(('rows', 'owners'), None, 'rep')
The draws below stay inside these ranges and needn't reach their ends.
Inputs may be any that keep to these rules, and one draw needn't show every extreme that they name: `columns`: row i's first entry is i itself; the entries of a row are distinct and each lies within 48 rows of i, modulo 6144 (the graph is periodic). The first row of every aligned block of 48 rows names the rows 48 before and after it. `aggregate`: never falls; the g-th aligned block of 48 fine rows names exactly the coarse rows g * 16 to g * 16 + 15, each by two or more rows, and aggregate[i] - g * 16 depends only on the position of i within its block, the same for every block. coarse_slots[i, k] is 16 plus the difference aggregate[columns[i, k]] - aggregate[i], taken modulo 2048 as the signed value of smallest magnitude.
All inputs are finite; a program needn't handle non-finite values.
Results may differ from the reference program's by a relative error of at most 0.0029.
Values may be sent and summed in bfloat16 or wider, within the bound.
A program may use at most 192 MiB of HBM per device.

```python
import jax
import jax.numpy as jnp
from jax import lax

BLOCK = 64
SLOTS = 27
ROWS_DEV = 48
GROUPS = 128
AGGS = 16
FINE = 6144
COARSE = 2048
CREACH = 16
CSLOTS = 33


def pattern(key):
    total_rows = ROWS_DEV * GROUPS
    window_size = 2 * ROWS_DEV + 1
    scores = jax.random.randint(jax.random.fold_in(key, 7), (total_rows, window_size), 0, 65536) * window_size
    window_ids = jnp.arange(window_size, dtype=jnp.int32)
    scores = scores + window_ids[None, :]
    row_ids = jnp.arange(total_rows, dtype=jnp.int32)
    is_self = window_ids[None, :] == ROWS_DEV
    is_first = jnp.mod(row_ids, ROWS_DEV)[:, None] == 0
    is_far = jnp.logical_or(window_ids[None, :] == 0, window_ids[None, :] == 2 * ROWS_DEV)
    forced = jnp.logical_and(is_first, is_far)
    scores = jnp.where(forced, 65536 * window_size + window_ids[None, :], scores)
    scores = jnp.where(is_self, 65536 * window_size + 2 * window_size, scores)
    _, chosen = lax.top_k(scores, SLOTS)
    col_ids = jnp.mod(row_ids[:, None] + chosen.astype(jnp.int32) - ROWS_DEV, total_rows).astype(jnp.int32)
    extras = jax.random.randint(jax.random.fold_in(key, 13), (AGGS,), 0, AGGS)
    counts = jnp.sum((extras[:, None] == jnp.arange(AGGS, dtype=jnp.int32)[None, :]).astype(jnp.int32), axis=0)
    ends = jnp.cumsum(2 + counts).astype(jnp.int32)
    positions = jnp.arange(ROWS_DEV, dtype=jnp.int32)
    local_agg = jnp.sum((ends[None, :] <= positions[:, None]).astype(jnp.int32), axis=1)
    agg_ids = (jnp.arange(GROUPS, dtype=jnp.int32)[:, None] * AGGS + local_agg[None, :]).reshape(-1).astype(jnp.int32)
    delta = agg_ids[col_ids] - agg_ids[:, None]
    delta = jnp.mod(delta + COARSE // 2, COARSE) - COARSE // 2
    slots = (delta + CREACH).astype(jnp.int32)
    return (col_ids, agg_ids, slots)


def draw_columns(key, part):
    return pattern(key)[0]


def draw_aggregate(key, part):
    return pattern(key)[1]


def draw_coarse_slots(key, part):
    return pattern(key)[2]


def level_of(rng, dims, cuts, least, high):
    level, own = 1.0, jax.random.fold_in(rng, 6)
    for axis_at, parts in cuts:
        draws = jnp.exp(jax.random.uniform(jax.random.fold_in(own, axis_at), (parts,), jnp.float32, least / len(cuts), high / len(cuts)))
        level = level * jnp.repeat(draws, dims[axis_at] // parts).reshape([-1 if axis == axis_at else 1 for axis in range(len(dims))])
    return level


def gaussian(key, extent, width, reach, shards=(), held_as=jnp.bfloat16):
    factor_of = level_of(key, extent, shards, -0.22, 0.18) if shards else 1.0
    values = jax.random.normal(key, extent, jnp.float32) * width * factor_of
    return jnp.minimum(jnp.maximum(values, -reach), reach).astype(held_as)


def setup_inputs(seed: int = 0) -> dict:
    streams_of = jax.random.split(jax.random.key(seed), 6)
    blocks = gaussian(streams_of[0], (FINE, SLOTS, BLOCK * BLOCK), BLOCK ** -0.5, 0.75, ((0, 128),))
    panels = gaussian(streams_of[1], (FINE, 2, BLOCK * BLOCK // 2), (BLOCK // 8) ** -0.5, 2.0, ((0, 128), (1, 2)))
    columns = draw_columns(jax.random.fold_in(streams_of[5], 71), 0)
    aggregate = draw_aggregate(jax.random.fold_in(streams_of[5], 71), 0)
    coarse_slots = draw_coarse_slots(jax.random.fold_in(streams_of[5], 71), 0)
    return {"blocks": blocks, "panels": panels, "columns": columns, "aggregate": aggregate, "coarse_slots": coarse_slots}


def reference(blocks, panels, columns, aggregate, coarse_slots):
    block_side = BLOCK
    half_width = BLOCK // 2
    full_panels = panels.reshape(FINE, 2, block_side, half_width)

    def group_terms(coarse_sum, group_index):
        first_row = group_index * ROWS_DEV
        matrices = lax.dynamic_slice_in_dim(blocks, first_row, ROWS_DEV, 0)
        matrices = matrices.reshape(ROWS_DEV, SLOTS, block_side, block_side).astype(jnp.float32)
        col_index = lax.dynamic_slice_in_dim(columns, first_row, ROWS_DEV, 0).reshape(-1).astype(jnp.int32)
        picked = jnp.take(full_panels, col_index, axis=0)
        picked = picked.reshape(ROWS_DEV, SLOTS, 2, block_side, half_width).astype(jnp.float32)
        product = jnp.einsum('ikab,ikhbc->ikhac', matrices, picked).astype(jnp.bfloat16)
        product = lax.optimization_barrier(product).astype(jnp.float32)
        own_panels = lax.dynamic_slice_in_dim(full_panels, first_row, ROWS_DEV, 0).astype(jnp.float32)
        triple = jnp.einsum('igad,ikhac->ikhgdc', own_panels, product)
        triple = triple.reshape(ROWS_DEV * SLOTS, 2, block_side * half_width)
        agg_rows = lax.dynamic_slice_in_dim(aggregate, first_row, ROWS_DEV, 0)
        slot_rows = lax.dynamic_slice_in_dim(coarse_slots, first_row, ROWS_DEV, 0)
        target = (agg_rows[:, None] * CSLOTS + slot_rows).reshape(-1).astype(jnp.int32)
        return coarse_sum.at[target].add(triple), None

    coarse_sum = jnp.zeros((COARSE * CSLOTS, 2, block_side * half_width), jnp.float32)
    coarse_sum, _ = lax.scan(group_terms, coarse_sum, jnp.arange(GROUPS, dtype=jnp.int32))
    return coarse_sum.reshape(COARSE, CSLOTS, 2, block_side * half_width)
```

```python
import jax
import jax.numpy as jnp
from jax import lax
from jax.experimental import pallas as pl
from jax.experimental.pallas import tpu as pltpu
from jax.sharding import PartitionSpec as P

BLOCK = 64
HALF = 32
SLOTS = 27
ROWS = 48
AGGS = 16
CSLOTS = 33
TILE = 16
TILES = ROWS // TILE
PART = 9
UNROLL = 3
CHUNK = 6
CHUNKS = AGGS * CSLOTS // 4 // CHUNK
F32 = jnp.float32
BF16 = jnp.bfloat16
NT = (((1,), (1,)), ((), ()))


def iota(shape, dim):
    return lax.broadcasted_iota(jnp.int32, shape, dim)


def one_hot(mask):
    return jnp.where(mask, 1.0, 0.0).astype(F32).astype(BF16)


def prepare(refs, rep, spread_ref, order_ref, pt_ref, pi_ref):
    shape = (512, 1024)
    row, lane = iota(shape, 0), iota(shape, 1)
    same = (row % 8) == (lane // 128)
    source = 4 * ((row // 8) % 16) + row // 128
    place = lane % 64
    spread_ref[...] = one_hot(same & (source == place))
    natural = 32 * ((place // 16) % 2) + 2 * (place % 16) + place // 32
    order_ref[...] = one_hot(same & (source == natural))

    left, own, right, other = refs

    def transposed(ref):
        parts = []
        for q in range(TILES):
            rows16 = ref[q * TILE:(q + 1) * TILE, :].astype(F32)
            for half in range(2):
                rows8 = rows16[half * 8:half * 8 + 8, :]
                stacked = jnp.concatenate([rows8[:, u * 128:(u + 1) * 128] for u in range(16)], axis=0)
                turned = stacked.T.astype(BF16)
                parts.append(jnp.concatenate([turned[r * 32:(r + 1) * 32, :] for r in range(4)], axis=1))
        return jnp.concatenate(parts, axis=0)

    def put(result, store):
        result = result.astype(BF16)
        for group in range(6):
            for j in range(8):
                store(group * 8 + j, result[group * 32:(group + 1) * 32, j * 128:(j + 1) * 128])

    for base, ref in ((0, left), (ROWS, own), (2 * ROWS, right)):
        lhs = transposed(ref)

        def store_pt(j, value, base=base):
            pt_ref[base + j] = value

        put(jnp.dot(lhs, spread_ref[...], preferred_element_type=F32), store_pt)
    for ref, half in ((own, rep), (other, 1 - rep)):
        lhs = transposed(ref)
        start = pl.multiple_of(half * HALF, HALF)

        def store_pi(i, value, start=start):
            pi_ref[i, pl.ds(start, HALF), :] = value[:, :64]

        put(jnp.dot(lhs, order_ref[...], preferred_element_type=F32), store_pi)


def relayout(blocks_ref, x_ref, perm_ref, tile, k):
    native = blocks_ref[k, tile * TILE:(tile + 1) * TILE, :]
    halves = []
    for high in range(2):
        halves.append(jnp.concatenate(
            [native[:, (high * 16 + t) * 128:(high * 16 + t + 1) * 128] for t in range(16)], axis=0))
    rhs = jnp.concatenate(halves, axis=1)
    result = jnp.dot(perm_ref[...], rhs, preferred_element_type=F32).astype(BF16)
    for i in range(TILE):
        x_ref[tile * TILE + i, k] = result[i * 16:(i + 1) * 16, :]


def kernel(cols_ref, target_ref, rep_ref, blocks_hbm, left_ref, own_ref, right_ref, other_ref, out_hbm,
           blocks_ref, x_ref, pt_ref, pi_ref, acc_ref, spread_ref, order_ref, perm_ref, turn_ref, out_ref,
           product_a, product_b, in_sems, out_sems):
    def fetch(tile, part):
        slots = pl.ds(part * PART, PART)
        rows = pl.ds(tile * TILE, TILE)
        return pltpu.make_async_copy(
            blocks_hbm.at[slots, rows, :], blocks_ref.at[slots, rows, :], in_sems.at[tile * 3 + part])

    for tile in range(TILES):
        for part in range(3):
            fetch(tile, part).start()

    prepare((left_ref, own_ref, right_ref, other_ref), rep_ref[0], spread_ref, order_ref, pt_ref, pi_ref)
    row, lane = iota((256, 256), 0), iota((256, 256), 1)
    perm_ref[...] = one_hot((row // 16 == lane % 16) & (row % 16 == lane // 16))

    @pl.loop(0, AGGS)
    def _(t):
        for s in range(CSLOTS):
            acc_ref[t * CSLOTS + s] = jnp.zeros((HALF, BLOCK), F32)

    for tile in range(TILES):
        for part in range(3):
            fetch(tile, part).wait()

            @pl.loop(0, PART // UNROLL)
            def _(q, tile=tile, part=part):
                for u in range(UNROLL):
                    relayout(blocks_ref, x_ref, perm_ref, tile, part * PART + q * UNROLL + u)

    first = iota((16, 128), 1) < 64

    def stage_one(row, product_ref):
        for k in range(SLOTS):
            x0 = x_ref[row, k, :, 0:128]
            x1 = x_ref[row, k, :, 128:256]
            zero = jnp.zeros_like(x0)
            weights = jnp.concatenate([
                jnp.where(first, x0, zero), jnp.where(first, x1, zero),
                jnp.where(first, zero, x0), jnp.where(first, zero, x1)], axis=0)
            lhs = pt_ref[cols_ref[k, row]]
            product_ref[k * HALF:(k + 1) * HALF, :] = lax.dot_general(
                lhs, weights, NT, preferred_element_type=F32).astype(BF16)

    def stage_two(row, product_ref):
        triple = lax.dot_general(product_ref[...], pi_ref[row], NT, preferred_element_type=F32)
        for k in range(SLOTS):
            at_tile = target_ref[k, row]
            acc_ref[at_tile] = acc_ref[at_tile] + triple[k * HALF:(k + 1) * HALF, :]

    stage_one(0, product_a)

    @pl.loop(0, ROWS // 2)
    def _(pair):
        row = pair * 2
        stage_one(row + 1, product_b)
        stage_two(row, product_a)
        stage_one(jnp.minimum(row + 2, ROWS - 1), product_a)
        stage_two(row + 1, product_b)

    def send(chunk):
        rows = pl.ds(pl.multiple_of(chunk * (CHUNK * 64), CHUNK * 64), CHUNK * 64)
        return pltpu.make_async_copy(out_ref.at[rows, :], out_hbm.at[rows, :], out_sems.at[chunk])

    @pl.loop(0, CHUNKS)
    def _(chunk):
        for g in range(CHUNK):
            tile = (chunk * CHUNK + g) * 4
            stacked = jnp.concatenate([acc_ref[tile + s] for s in range(4)], axis=0)
            turn_ref[g] = stacked.T
            parts = [turn_ref[g, pl.ds(r, 16, stride=4), :] for r in range(4)]
            for s in range(4):
                pieces = [p[:, s * 32:(s + 1) * 32] for p in parts]
                where = pl.multiple_of((tile + s) * 16, 16)
                out_ref[pl.ds(where, 16), :] = jnp.concatenate(pieces, axis=1)
        send(chunk).start()

    @pl.loop(0, CHUNKS)
    def _(chunk):
        send(chunk).wait()


def local(cols, target, rep, blocks, left, own, right, other):
    vmem = pl.BlockSpec(memory_space=pltpu.VMEM)
    smem = pl.BlockSpec(memory_space=pltpu.SMEM)
    hbm = pl.BlockSpec(memory_space=pl.ANY)
    return pl.pallas_call(
        kernel,
        out_shape=jax.ShapeDtypeStruct((AGGS * CSLOTS * 16, 128), F32),
        in_specs=[smem, smem, smem, hbm, vmem, vmem, vmem, vmem],
        out_specs=hbm,
        scratch_shapes=[
            pltpu.VMEM((SLOTS, ROWS, BLOCK * BLOCK), BF16),
            pltpu.VMEM((ROWS, SLOTS, 16, 256), BF16),
            pltpu.VMEM((3 * ROWS, HALF, 128), BF16),
            pltpu.VMEM((ROWS, BLOCK, BLOCK), BF16),
            pltpu.VMEM((AGGS * CSLOTS, HALF, BLOCK), F32),
            pltpu.VMEM((512, 1024), BF16),
            pltpu.VMEM((512, 1024), BF16),
            pltpu.VMEM((256, 256), BF16),
            pltpu.VMEM((CHUNK, 64, 128), F32),
            pltpu.VMEM((AGGS * CSLOTS * 16, 128), F32),
            pltpu.VMEM((SLOTS * HALF, BLOCK), BF16),
            pltpu.VMEM((SLOTS * HALF, BLOCK), BF16),
            pltpu.SemaphoreType.DMA((9,)),
            pltpu.SemaphoreType.DMA((CHUNKS,)),
        ],
        compiler_params=pltpu.CompilerParams(vmem_limit_bytes=60 << 20),
        name="galerkin",
    )(cols, target, rep, blocks, left, own, right, other)


def shards(blocks, panels, columns, aggregate, coarse_slots):
    group = lax.axis_index(("rows", "owners"))
    groups = lax.axis_size(("rows", "owners"))
    total_rows = ROWS * groups
    own = panels.reshape(ROWS, 2048)
    up = [(i, (i + 1) % groups) for i in range(groups)]
    down = [(j, i) for i, j in up]
    left = lax.ppermute(own, ("rows", "owners"), up)
    right = lax.ppermute(own, ("rows", "owners"), down)
    other = lax.ppermute(own, "rep", [(0, 1), (1, 0)])
    cols = jnp.mod(columns.T - group * ROWS + ROWS, total_rows)
    target = (aggregate - group * AGGS)[None, :] * CSLOTS + coarse_slots.T
    rep = lax.axis_index("rep").reshape(1)
    out = local(cols, target, rep, jnp.transpose(blocks, (1, 0, 2)), left, own, right, other)
    return out.reshape(AGGS, CSLOTS, 1, 2048)


def solution(mesh):
    return jax.shard_map(
        shards,
        mesh=mesh,
        in_specs=(
            P(("rows", "owners"), None, None),
            P(("rows", "owners"), "rep", None),
            P(("rows", "owners"), None),
            P(("rows", "owners")),
            P(("rows", "owners"), None),
        ),
        out_specs=P(("rows", "owners"), None, "rep", None),
        check_vma=False,
    )
```

```python
import jax
import jax.numpy as jnp
from jax import lax
from jax.experimental import pallas as pl
from jax.experimental.pallas import tpu as pltpu
from jax.sharding import PartitionSpec as P

BLOCK = 64
HALF = 32
SLOTS = 27
ROWS = 48
AGGS = 16
CSLOTS = 33
TILE = 16
TILES = ROWS // TILE
PART = 9
QUADS = 7
CHUNK = 12
CHUNKS = AGGS * CSLOTS // 4 // CHUNK
F32 = jnp.float32
BF16 = jnp.bfloat16
NT = (((1,), (1,)), ((), ()))


def iota(shape, dim):
    return lax.broadcasted_iota(jnp.int32, shape, dim)


def one_hot(mask):
    return jnp.where(mask, 1.0, 0.0).astype(F32).astype(BF16)


def prepare(refs, rep, spread_ref, order_ref, pt_ref, pi_ref):
    def table(width, place_of):
        row, lane = iota((512, 8 * width), 0), iota((512, 8 * width), 1)
        same = (row % 8) == (lane // width)
        source = 4 * ((row // 8) % 16) + row // 128
        return one_hot(same & (source == place_of(lane % width)))

    spread_ref[...] = table(128, lambda p: p % 64)
    order_ref[...] = table(256, lambda p: 32 * ((p // 16) % 2) + 2 * (p % 16) + p // 128)

    left, own, right, other = refs

    def transposed(ref):
        parts = []
        for q in range(TILES):
            rows16 = ref[q * TILE:(q + 1) * TILE, :].astype(F32)
            for half in range(2):
                rows8 = rows16[half * 8:half * 8 + 8, :]
                stacked = jnp.concatenate([rows8[:, u * 128:(u + 1) * 128] for u in range(16)], axis=0)
                turned = stacked.T.astype(BF16)
                parts.append(jnp.concatenate([turned[r * 32:(r + 1) * 32, :] for r in range(4)], axis=1))
        return jnp.concatenate(parts, axis=0)

    def put(result, width, store):
        result = result.astype(BF16)
        for group in range(6):
            for j in range(8):
                store(group * 8 + j, result[group * 32:(group + 1) * 32, j * width:(j + 1) * width])

    first = iota((HALF, 128), 1) < 64
    for base, ref in ((0, left), (ROWS, own), (2 * ROWS, right)):
        lhs = transposed(ref)

        def store_pt(j, value, base=base):
            zero = jnp.zeros_like(value)
            pt_ref[base + j, 0:HALF, :] = jnp.where(first, value, zero)
            pt_ref[base + j, HALF:BLOCK, :] = jnp.where(first, zero, value)

        put(jnp.dot(lhs, spread_ref[...], preferred_element_type=F32), 128, store_pt)
    for ref, half in ((own, rep), (other, 1 - rep)):
        lhs = transposed(ref)
        start = pl.multiple_of(half * HALF, HALF)

        def store_pi(i, value, start=start):
            pi_ref[i, 0, pl.ds(start, HALF), :] = value[:, 0:128]
            pi_ref[i, 1, pl.ds(start, HALF), :] = value[:, 128:256]

        put(jnp.dot(lhs, order_ref[...], preferred_element_type=F32), 256, store_pi)


def relayout(blocks_ref, x_ref, perm_ref, tile, k):
    native = blocks_ref[k, pl.ds(pl.multiple_of(tile * TILE, TILE), TILE), :]
    halves = []
    for high in range(2):
        halves.append(jnp.concatenate(
            [native[:, (high * 16 + t) * 128:(high * 16 + t + 1) * 128] for t in range(16)], axis=0))
    rhs = jnp.concatenate(halves, axis=1)
    result = jnp.dot(perm_ref[...], rhs, preferred_element_type=F32).astype(BF16)
    for i in range(TILE):
        x_ref[tile * TILE + i, k, 0:16, :] = result[i * 16:(i + 1) * 16, 0:128]
        x_ref[tile * TILE + i, k, 16:32, :] = result[i * 16:(i + 1) * 16, 128:256]


def products(x_ref, pt_ref, cols_ref, row, product_ref):
    zero = jnp.zeros((HALF, 128), BF16)

    def pair(k0, k1):
        lhs = jnp.concatenate([pt_ref[cols_ref[k0, row]], pt_ref[cols_ref[k1, row]]], axis=1)
        weights = jnp.concatenate([
            jnp.concatenate([x_ref[row, k0], zero], axis=1),
            jnp.concatenate([zero, x_ref[row, k1]], axis=1)], axis=0)
        return lax.dot_general(lhs, weights, NT, preferred_element_type=F32).astype(BF16)

    for group in range(QUADS):
        k = [min(group * 4 + n, SLOTS - 1) for n in range(4)]
        both = jnp.concatenate([pair(k[0], k[1]), pair(k[2], k[3])], axis=1)
        rows = slice(group * HALF, (group + 1) * HALF)
        product_ref[0, rows, :] = both[0:HALF]
        product_ref[1, rows, :] = both[HALF:BLOCK]


def accumulate(pi_ref, target_ref, row, product_ref, acc_ref):
    block = iota((BLOCK, 128), 1) // 32
    even, odd = pi_ref[row, 0], pi_ref[row, 1]
    zero = jnp.zeros_like(even)
    weights = jnp.concatenate([
        jnp.concatenate([jnp.where(block == n, even, zero), jnp.where(block == n, odd, zero)], axis=1)
        for n in range(4)], axis=0)
    lhs = jnp.concatenate([product_ref[0], product_ref[1]], axis=1)
    triple = lax.dot_general(lhs, weights, NT, preferred_element_type=F32)
    for k in range(SLOTS):
        group, n = divmod(k, 4)
        at = target_ref[k, row]
        lanes = slice((n % 2) * BLOCK, (n % 2 + 1) * BLOCK)
        value = triple[group * HALF:(group + 1) * HALF, n * BLOCK:(n + 1) * BLOCK]
        acc_ref[at, :, lanes] = acc_ref[at, :, lanes] + value


def finish(acc_ref, fold_ref, out_ref, tile):
    stacked = jnp.concatenate([acc_ref[tile + s] for s in range(4)], axis=0)
    head = stacked.astype(BF16)
    tail = (stacked - head.astype(F32)).astype(BF16)
    turned = lax.dot_general(
        fold_ref[...], jnp.concatenate([head, tail], axis=1), NT, preferred_element_type=F32)
    p = [turned[r * 16:(r + 1) * 16] for r in range(4)]
    lane = iota((16, 128), 1)
    low, even = lane < 64, lane % 64 < 32
    u = [jnp.where(low, p[0], pltpu.roll(p[2], 64, 1)), jnp.where(low, p[1], pltpu.roll(p[3], 64, 1)),
         jnp.where(low, pltpu.roll(p[0], 64, 1), p[2]), jnp.where(low, pltpu.roll(p[1], 64, 1), p[3])]
    for s in range(4):
        a, b = u[s // 2 * 2], u[s // 2 * 2 + 1]
        value = jnp.where(even, a, pltpu.roll(b, 32, 1)) if s % 2 == 0 else jnp.where(even, pltpu.roll(a, 96, 1), b)
        out_ref[pl.ds(pl.multiple_of((tile + s) * 16, 16), 16), :] = value


def kernel(cols_ref, target_ref, rep_ref, blocks_hbm, left_ref, own_ref, right_ref, other_ref, out_hbm,
           blocks_ref, x_ref, pt_ref, pi_ref, acc_ref, spread_ref, order_ref, perm_ref, fold_ref, out_ref,
           product_a, product_b, in_sems, out_sems):
    def fetch(part):
        slots = pl.ds(part % 3 * PART, PART)
        rows = pl.ds(pl.multiple_of(part // 3 * TILE, TILE), TILE)
        return pltpu.make_async_copy(
            blocks_hbm.at[slots, rows, :], blocks_ref.at[slots, rows, :], in_sems.at[part])

    for part in range(9):
        fetch(part).start()

    prepare((left_ref, own_ref, right_ref, other_ref), rep_ref[0], spread_ref, order_ref, pt_ref, pi_ref)
    row, lane = iota((256, 256), 0), iota((256, 256), 1)
    perm_ref[...] = one_hot((row // 16 == lane % 16) & (row % 16 == lane // 16))
    row, lane = iota((BLOCK, 256), 0), iota((BLOCK, 256), 1)
    fold_ref[...] = one_hot(4 * (row % 16) + row // 16 == lane % 64)

    @pl.loop(0, AGGS)
    def _(t):
        for s in range(CSLOTS):
            acc_ref[t * CSLOTS + s] = jnp.zeros((HALF, 128), F32)

    @pl.loop(0, 9)
    def _(part):
        fetch(part).wait()
        for q in range(PART):
            relayout(blocks_ref, x_ref, perm_ref, part // 3, part % 3 * PART + q)

    products(x_ref, pt_ref, cols_ref, 0, product_a)

    @pl.loop(0, ROWS // 2)
    def _(pair):
        row = pair * 2
        products(x_ref, pt_ref, cols_ref, row + 1, product_b)
        accumulate(pi_ref, target_ref, row, product_a, acc_ref)
        products(x_ref, pt_ref, cols_ref, jnp.minimum(row + 2, ROWS - 1), product_a)
        accumulate(pi_ref, target_ref, row + 1, product_b, acc_ref)

    def send(chunk):
        rows = pl.ds(pl.multiple_of(chunk * (CHUNK * 64), CHUNK * 64), CHUNK * 64)
        return pltpu.make_async_copy(out_ref.at[rows, :], out_hbm.at[rows, :], out_sems.at[chunk])

    @pl.loop(0, CHUNKS)
    def _(chunk):
        for g in range(CHUNK):
            finish(acc_ref, fold_ref, out_ref, (chunk * CHUNK + g) * 4)
        send(chunk).start()

    @pl.loop(0, CHUNKS)
    def _(chunk):
        send(chunk).wait()


def local(cols, target, rep, blocks, left, own, right, other):
    vmem = pl.BlockSpec(memory_space=pltpu.VMEM)
    smem = pl.BlockSpec(memory_space=pltpu.SMEM)
    hbm = pl.BlockSpec(memory_space=pl.ANY)
    return pl.pallas_call(
        kernel,
        out_shape=jax.ShapeDtypeStruct((AGGS * CSLOTS * 16, 128), F32),
        in_specs=[smem, smem, smem, hbm, vmem, vmem, vmem, vmem],
        out_specs=hbm,
        scratch_shapes=[
            pltpu.VMEM((SLOTS, ROWS, BLOCK * BLOCK), BF16),
            pltpu.VMEM((ROWS, SLOTS, HALF, 128), BF16),
            pltpu.VMEM((3 * ROWS, BLOCK, 128), BF16),
            pltpu.VMEM((ROWS, 2, BLOCK, 128), BF16),
            pltpu.VMEM((AGGS * CSLOTS, HALF, 128), F32),
            pltpu.VMEM((512, 1024), BF16),
            pltpu.VMEM((512, 2048), BF16),
            pltpu.VMEM((256, 256), BF16),
            pltpu.VMEM((BLOCK, 256), BF16),
            pltpu.VMEM((AGGS * CSLOTS * 16, 128), F32),
            pltpu.VMEM((2, QUADS * HALF, 128), BF16),
            pltpu.VMEM((2, QUADS * HALF, 128), BF16),
            pltpu.SemaphoreType.DMA((9,)),
            pltpu.SemaphoreType.DMA((CHUNKS,)),
        ],
        compiler_params=pltpu.CompilerParams(vmem_limit_bytes=60 << 20),
        name="galerkin",
    )(cols, target, rep, blocks, left, own, right, other)


def shards(blocks, panels, columns, aggregate, coarse_slots):
    group = lax.axis_index(("rows", "owners"))
    groups = lax.axis_size(("rows", "owners"))
    total_rows = ROWS * groups
    own = panels.reshape(ROWS, 2048)
    up = [(i, (i + 1) % groups) for i in range(groups)]
    down = [(j, i) for i, j in up]
    left = lax.ppermute(own, ("rows", "owners"), up)
    right = lax.ppermute(own, ("rows", "owners"), down)
    other = lax.ppermute(own, "rep", [(0, 1), (1, 0)])
    cols = jnp.mod(columns.T - group * ROWS + ROWS, total_rows)
    target = (aggregate - group * AGGS)[None, :] * CSLOTS + coarse_slots.T
    rep = lax.axis_index("rep").reshape(1)
    out = local(cols, target, rep, jnp.transpose(blocks, (1, 0, 2)), left, own, right, other)
    return out.reshape(AGGS, CSLOTS, 1, 2048)


def solution(mesh):
    return jax.shard_map(
        shards,
        mesh=mesh,
        in_specs=(
            P(("rows", "owners"), None, None),
            P(("rows", "owners"), "rep", None),
            P(("rows", "owners"), None),
            P(("rows", "owners")),
            P(("rows", "owners"), None),
        ),
        out_specs=P(("rows", "owners"), None, "rep", None),
        check_vma=False,
    )
```

```python
import jax
import jax.numpy as jnp
from jax import lax
from jax.experimental import pallas as pl
from jax.experimental.pallas import tpu as pltpu
from jax.sharding import PartitionSpec as P

BLOCK = 64
HALF = 32
SLOTS = 27
ROWS = 48
AGGS = 16
CSLOTS = 33
TILE = 16
TILES = ROWS // TILE
PART = 9
EARLY = 2
FETCH = 8
FINE = 6144
QUADS = 7
CHUNK = 12
CHUNKS = AGGS * CSLOTS // 4 // CHUNK
F32 = jnp.float32
BF16 = jnp.bfloat16
NT = (((1,), (1,)), ((), ()))


def iota(shape, dim):
    return lax.broadcasted_iota(jnp.int32, shape, dim)


def one_hot(mask):
    return jnp.where(mask, 1.0, 0.0).astype(F32).astype(BF16)


def prepare(refs, rep, spread_ref, order_ref, pt_ref, pi_ref):
    def table(width, place_of):
        row, lane = iota((512, 8 * width), 0), iota((512, 8 * width), 1)
        same = (row % 8) == (lane // width)
        source = 4 * ((row // 8) % 16) + row // 128
        return one_hot(same & (source == place_of(lane % width)))

    spread_ref[...] = table(128, lambda p: p % 64)
    order_ref[...] = table(256, lambda p: 32 * ((p // 16) % 2) + 2 * (p % 16) + p // 128)

    left, own, right, other = refs

    def transposed(ref):
        parts = []
        for q in range(TILES):
            rows16 = ref[q * TILE:(q + 1) * TILE, :].astype(F32)
            for half in range(2):
                rows8 = rows16[half * 8:half * 8 + 8, :]
                stacked = jnp.concatenate([rows8[:, u * 128:(u + 1) * 128] for u in range(16)], axis=0)
                turned = stacked.T.astype(BF16)
                parts.append(jnp.concatenate([turned[r * 32:(r + 1) * 32, :] for r in range(4)], axis=1))
        return jnp.concatenate(parts, axis=0)

    def put(result, width, store):
        result = result.astype(BF16)
        for group in range(6):
            for j in range(8):
                store(group * 8 + j, result[group * 32:(group + 1) * 32, j * width:(j + 1) * width])

    first = iota((HALF, 128), 1) < 64
    for base, ref in ((0, left), (ROWS, own), (2 * ROWS, right)):
        lhs = transposed(ref)

        def store_pt(j, value, base=base):
            zero = jnp.zeros_like(value)
            pt_ref[base + j, 0:HALF, :] = jnp.where(first, value, zero)
            pt_ref[base + j, HALF:BLOCK, :] = jnp.where(first, zero, value)

        put(jnp.dot(lhs, spread_ref[...], preferred_element_type=F32), 128, store_pt)
    for ref, half in ((own, rep), (other, 1 - rep)):
        lhs = transposed(ref)
        start = pl.multiple_of(half * HALF, HALF)

        def store_pi(i, value, start=start):
            pi_ref[i, 0, pl.ds(start, HALF), :] = value[:, 0:128]
            pi_ref[i, 1, pl.ds(start, HALF), :] = value[:, 128:256]

        put(jnp.dot(lhs, order_ref[...], preferred_element_type=F32), 256, store_pi)


def relayout(blocks_ref, x_ref, perm_ref, tile, k):
    native = blocks_ref[k, pl.ds(pl.multiple_of(tile * TILE, TILE), TILE), :]
    halves = []
    for high in range(2):
        halves.append(jnp.concatenate(
            [native[:, (high * 16 + t) * 128:(high * 16 + t + 1) * 128] for t in range(16)], axis=0))
    rhs = jnp.concatenate(halves, axis=1)
    result = jnp.dot(perm_ref[...], rhs, preferred_element_type=F32).astype(BF16)
    for i in range(TILE):
        x_ref[tile * TILE + i, k, 0:16, :] = result[i * 16:(i + 1) * 16, 0:128]
        x_ref[tile * TILE + i, k, 16:32, :] = result[i * 16:(i + 1) * 16, 128:256]


def products(x_ref, pt_ref, column, row, product_ref):
    zero = jnp.zeros((HALF, 128), BF16)

    def pair(k0, k1):
        lhs = jnp.concatenate([pt_ref[column(k0, row)], pt_ref[column(k1, row)]], axis=1)
        weights = jnp.concatenate([
            jnp.concatenate([x_ref[row, k0], zero], axis=1),
            jnp.concatenate([zero, x_ref[row, k1]], axis=1)], axis=0)
        return lax.dot_general(lhs, weights, NT, preferred_element_type=F32).astype(BF16)

    for group in range(QUADS):
        k = [min(group * 4 + n, SLOTS - 1) for n in range(4)]
        both = jnp.concatenate([pair(k[0], k[1]), pair(k[2], k[3])], axis=1)
        rows = slice(group * HALF, (group + 1) * HALF)
        product_ref[0, rows, :] = both[0:HALF]
        product_ref[1, rows, :] = both[HALF:BLOCK]


def accumulate(pi_ref, place, row, product_ref, acc_ref):
    block = iota((BLOCK, 128), 1) // 32
    even, odd = pi_ref[row, 0], pi_ref[row, 1]
    zero = jnp.zeros_like(even)
    weights = jnp.concatenate([
        jnp.concatenate([jnp.where(block == n, even, zero), jnp.where(block == n, odd, zero)], axis=1)
        for n in range(4)], axis=0)
    lhs = jnp.concatenate([product_ref[0], product_ref[1]], axis=1)
    triple = lax.dot_general(lhs, weights, NT, preferred_element_type=F32)
    for k in range(SLOTS):
        group, n = divmod(k, 4)
        at = place(k, row)
        lanes = slice((n % 2) * BLOCK, (n % 2 + 1) * BLOCK)
        value = triple[group * HALF:(group + 1) * HALF, n * BLOCK:(n + 1) * BLOCK]
        acc_ref[at, :, lanes] = acc_ref[at, :, lanes] + value


def finish(acc_ref, fold_ref, out_ref, tile):
    stacked = jnp.concatenate([acc_ref[tile + s] for s in range(4)], axis=0)
    head = stacked.astype(BF16)
    tail = (stacked - head.astype(F32)).astype(BF16)
    turned = lax.dot_general(
        fold_ref[...], jnp.concatenate([head, tail], axis=1), NT, preferred_element_type=F32)
    p = [turned[r * 16:(r + 1) * 16] for r in range(4)]
    lane = iota((16, 128), 1)
    low, even = lane < 64, lane % 64 < 32
    u = [jnp.where(low, p[0], pltpu.roll(p[2], 64, 1)), jnp.where(low, p[1], pltpu.roll(p[3], 64, 1)),
         jnp.where(low, pltpu.roll(p[0], 64, 1), p[2]), jnp.where(low, pltpu.roll(p[1], 64, 1), p[3])]
    for s in range(4):
        a, b = u[s // 2 * 2], u[s // 2 * 2 + 1]
        value = jnp.where(even, a, pltpu.roll(b, 32, 1)) if s % 2 == 0 else jnp.where(even, pltpu.roll(a, 96, 1), b)
        out_ref[pl.ds(pl.multiple_of((tile + s) * 16, 16), 16), :] = value


def exchange_kernel(blocks_hbm, own_hbm, x_hbm, left_hbm, right_hbm, other_hbm,
                    blocks_ref, x_ref, perm_ref, in_sems, out_sems, send_sems, recv_sems):
    r, o, c = lax.axis_index("rows"), lax.axis_index("owners"), lax.axis_index("rep")
    rows, owners = lax.axis_size("rows"), lax.axis_size("owners")
    groups = rows * owners
    group = r * owners + o
    after, before = (group + 1) % groups, (group + groups - 1) % groups
    targets = [(after // owners, after % owners, c), (before // owners, before % owners, c), (r, o, 1 - c)]
    barrier = pltpu.get_barrier_semaphore()
    for target in targets:
        pl.semaphore_signal(barrier, inc=1, device_id=target, device_id_type=pl.DeviceIdType.MESH)

    def pieces(part):
        return pl.ds(pl.multiple_of(part // 3 * TILE, TILE), TILE), pl.ds(part % 3 * PART, PART)

    def fetch(part):
        rows_at, slots_at = pieces(part)
        return pltpu.make_async_copy(
            blocks_hbm.at[slots_at, rows_at, :], blocks_ref.at[slots_at, rows_at, :], in_sems.at[part])

    def keep(part):
        rows_at, slots_at = pieces(part)
        return pltpu.make_async_copy(x_ref.at[rows_at, slots_at], x_hbm.at[rows_at, slots_at], out_sems.at[part])

    for part in range(9):
        fetch(part).start()
    row, lane = iota((256, 256), 0), iota((256, 256), 1)
    perm_ref[...] = one_hot((row // 16 == lane % 16) & (row % 16 == lane // 16))

    def turn(part, _):
        fetch(part).wait()
        for q in range(PART):
            relayout(blocks_ref, x_ref, perm_ref, part // 3, part % 3 * PART + q)
        keep(part).start()
        return 0

    lax.fori_loop(0, EARLY, turn, 0)
    pl.semaphore_wait(barrier, 3)
    copies = []
    for n, (target, landing) in enumerate(zip(targets, (left_hbm, right_hbm, other_hbm))):
        copies.append(pltpu.make_async_remote_copy(
            src_ref=own_hbm, dst_ref=landing, send_sem=send_sems.at[n], recv_sem=recv_sems.at[n],
            device_id=target, device_id_type=pl.DeviceIdType.MESH))
    for copy in copies:
        copy.start()
    lax.fori_loop(EARLY, 9, turn, 0)
    for part in range(9):
        keep(part).wait()
    for copy in copies:
        copy.wait()


def exchange(blocks, own):
    anywhere = pl.BlockSpec(memory_space=pl.ANY)
    panel = jax.ShapeDtypeStruct((ROWS, 2048), BF16)
    return pl.pallas_call(
        exchange_kernel,
        out_shape=(jax.ShapeDtypeStruct((ROWS, SLOTS, HALF, 128), BF16), panel, panel, panel),
        in_specs=[anywhere, anywhere],
        out_specs=(anywhere, anywhere, anywhere, anywhere),
        scratch_shapes=[
            pltpu.VMEM((SLOTS, ROWS, BLOCK * BLOCK), BF16),
            pltpu.VMEM((ROWS, SLOTS, HALF, 128), BF16),
            pltpu.VMEM((256, 256), BF16),
            pltpu.SemaphoreType.DMA((9,)),
            pltpu.SemaphoreType.DMA((9,)),
            pltpu.SemaphoreType.DMA((3,)),
            pltpu.SemaphoreType.DMA((3,)),
        ],
        compiler_params=pltpu.CompilerParams(
            vmem_limit_bytes=60 << 20, collective_id=0, has_side_effects=True),
        name="turn_blocks",
    )(blocks, own)


def kernel(cols_ref, slots_ref, agg_ref, x_hbm, left_ref, own_ref, right_ref, other_ref, out_hbm,
           x_ref, pt_ref, pi_ref, acc_ref, spread_ref, order_ref, fold_ref, out_ref,
           product_a, product_b, in_sems, out_sems):
    group = lax.axis_index("rows") * lax.axis_size("owners") + lax.axis_index("owners")
    first_row, first_coarse = group * ROWS, group * AGGS

    def fetch(part):
        rows = pl.ds(part * FETCH, FETCH)
        return pltpu.make_async_copy(x_hbm.at[rows], x_ref.at[rows], in_sems.at[part])

    for part in range(ROWS // FETCH):
        fetch(part).start()

    prepare((left_ref, own_ref, right_ref, other_ref), lax.axis_index("rep"), spread_ref, order_ref, pt_ref, pi_ref)
    row, lane = iota((BLOCK, 256), 0), iota((BLOCK, 256), 1)
    fold_ref[...] = one_hot(4 * (row % 16) + row // 16 == lane % 64)

    @pl.loop(0, AGGS)
    def _(t):
        for s in range(CSLOTS):
            acc_ref[t * CSLOTS + s] = jnp.zeros((HALF, 128), F32)

    for part in range(ROWS // FETCH):
        fetch(part).wait()

    def column(k, row):
        near = cols_ref[k, row] - first_row + ROWS
        near = jnp.where(near < 0, near + FINE, near)
        return jnp.where(near >= FINE, near - FINE, near)

    def place(k, row):
        return (agg_ref[row] - first_coarse) * CSLOTS + slots_ref[k, row]

    products(x_ref, pt_ref, column, 0, product_a)

    @pl.loop(0, ROWS // 2)
    def _(pair):
        row = pair * 2
        products(x_ref, pt_ref, column, row + 1, product_b)
        accumulate(pi_ref, place, row, product_a, acc_ref)
        products(x_ref, pt_ref, column, jnp.minimum(row + 2, ROWS - 1), product_a)
        accumulate(pi_ref, place, row + 1, product_b, acc_ref)

    def send(chunk):
        rows = pl.ds(pl.multiple_of(chunk * (CHUNK * 64), CHUNK * 64), CHUNK * 64)
        return pltpu.make_async_copy(out_ref.at[rows, :], out_hbm.at[rows, :], out_sems.at[chunk])

    @pl.loop(0, CHUNKS)
    def _(chunk):
        for g in range(CHUNK):
            finish(acc_ref, fold_ref, out_ref, (chunk * CHUNK + g) * 4)
        send(chunk).start()

    @pl.loop(0, CHUNKS)
    def _(chunk):
        send(chunk).wait()


def combine(cols, slots, agg, x, left, own, right, other):
    vmem = pl.BlockSpec(memory_space=pltpu.VMEM)
    smem = pl.BlockSpec(memory_space=pltpu.SMEM)
    anywhere = pl.BlockSpec(memory_space=pl.ANY)
    return pl.pallas_call(
        kernel,
        out_shape=jax.ShapeDtypeStruct((AGGS * CSLOTS * 16, 128), F32),
        in_specs=[smem, smem, smem, anywhere, vmem, vmem, vmem, vmem],
        out_specs=anywhere,
        scratch_shapes=[
            pltpu.VMEM((ROWS, SLOTS, HALF, 128), BF16),
            pltpu.VMEM((3 * ROWS, BLOCK, 128), BF16),
            pltpu.VMEM((ROWS, 2, BLOCK, 128), BF16),
            pltpu.VMEM((AGGS * CSLOTS, HALF, 128), F32),
            pltpu.VMEM((512, 1024), BF16),
            pltpu.VMEM((512, 2048), BF16),
            pltpu.VMEM((BLOCK, 256), BF16),
            pltpu.VMEM((AGGS * CSLOTS * 16, 128), F32),
            pltpu.VMEM((2, QUADS * HALF, 128), BF16),
            pltpu.VMEM((2, QUADS * HALF, 128), BF16),
            pltpu.SemaphoreType.DMA((ROWS // FETCH,)),
            pltpu.SemaphoreType.DMA((CHUNKS,)),
        ],
        compiler_params=pltpu.CompilerParams(vmem_limit_bytes=60 << 20),
        name="galerkin",
    )(cols, slots, agg, x, left, own, right, other)


def shards(blocks, panels, columns, aggregate, coarse_slots):
    own = panels.reshape(ROWS, 2048)
    x, left, right, other = exchange(jnp.transpose(blocks, (1, 0, 2)), own)
    out = combine(columns.T, coarse_slots.T, aggregate, x, left, own, right, other)
    return out.reshape(AGGS, CSLOTS, 1, 2048)


def solution(mesh):
    return jax.shard_map(
        shards,
        mesh=mesh,
        in_specs=(
            P(("rows", "owners"), None, None),
            P(("rows", "owners"), "rep", None),
            P(("rows", "owners"), None),
            P(("rows", "owners")),
            P(("rows", "owners"), None),
        ),
        out_specs=P(("rows", "owners"), None, "rep", None),
        check_vma=False,
    )
```

```python
import jax
import jax.numpy as jnp
from jax import lax
from jax.experimental import pallas as pl
from jax.experimental.pallas import tpu as pltpu
from jax.sharding import PartitionSpec as P

BLOCK = 64
HALF = 32
SLOTS = 27
ROWS = 48
AGGS = 16
CSLOTS = 33
TILE = 16
TILES = ROWS // TILE
PART = 9
EARLY = 2
STEP = 8
FETCH = STEP
FINE = 6144
QUADS = 7
CHUNK = 22
CHUNKS = AGGS * CSLOTS // 4 // CHUNK
F32 = jnp.float32
BF16 = jnp.bfloat16
NT = (((1,), (1,)), ((), ()))


def iota(shape, dim):
    return lax.broadcasted_iota(jnp.int32, shape, dim)


def one_hot(mask):
    return jnp.where(mask, 1.0, 0.0).astype(F32).astype(BF16)


def prepare(refs, rep, spread_ref, order_ref, pt_ref, pi_ref):
    def table(width, place_of):
        row, lane = iota((512, 8 * width), 0), iota((512, 8 * width), 1)
        same = (row % 8) == (lane // width)
        source = 4 * ((row // 8) % 16) + row // 128
        return one_hot(same & (source == place_of(lane % width)))

    spread_ref[...] = table(128, lambda p: p % 64)
    order_ref[...] = table(256, lambda p: 32 * ((p // 16) % 2) + 2 * (p % 16) + p // 128)

    left, own, right, other = refs

    def transposed(ref):
        parts = []
        for q in range(TILES):
            rows16 = ref[q * TILE:(q + 1) * TILE, :].astype(F32)
            for half in range(2):
                rows8 = rows16[half * 8:half * 8 + 8, :]
                stacked = jnp.concatenate([rows8[:, u * 128:(u + 1) * 128] for u in range(16)], axis=0)
                turned = stacked.T.astype(BF16)
                parts.append(jnp.concatenate([turned[r * 32:(r + 1) * 32, :] for r in range(4)], axis=1))
        return jnp.concatenate(parts, axis=0)

    def put(result, width, store):
        result = result.astype(BF16)
        for group in range(6):
            for j in range(8):
                store(group * 8 + j, result[group * 32:(group + 1) * 32, j * width:(j + 1) * width])

    first = iota((HALF, 128), 1) < 64
    for base, ref in ((0, left), (ROWS, own), (2 * ROWS, right)):
        lhs = transposed(ref)

        def store_pt(j, value, base=base):
            zero = jnp.zeros_like(value)
            pt_ref[base + j, 0:HALF, :] = jnp.where(first, value, zero)
            pt_ref[base + j, HALF:BLOCK, :] = jnp.where(first, zero, value)

        put(jnp.dot(lhs, spread_ref[...], preferred_element_type=F32), 128, store_pt)
    for ref, half in ((own, rep), (other, 1 - rep)):
        lhs = transposed(ref)
        start = pl.multiple_of(half * HALF, HALF)

        def store_pi(i, value, start=start):
            pi_ref[i, 0, pl.ds(start, HALF), :] = value[:, 0:128]
            pi_ref[i, 1, pl.ds(start, HALF), :] = value[:, 128:256]

        put(jnp.dot(lhs, order_ref[...], preferred_element_type=F32), 256, store_pi)


def relayout(blocks_ref, x_ref, perm_ref, tile, k):
    native = blocks_ref[k, pl.ds(pl.multiple_of(tile * TILE, TILE), TILE), :]
    halves = []
    for high in range(2):
        halves.append(jnp.concatenate(
            [native[:, (high * 16 + t) * 128:(high * 16 + t + 1) * 128] for t in range(16)], axis=0))
    rhs = jnp.concatenate(halves, axis=1)
    result = jnp.dot(perm_ref[...], rhs, preferred_element_type=F32).astype(BF16)
    for i in range(TILE):
        x_ref[tile * TILE + i, k, 0:16, :] = result[i * 16:(i + 1) * 16, 0:128]
        x_ref[tile * TILE + i, k, 16:32, :] = result[i * 16:(i + 1) * 16, 128:256]


def products(x_ref, pt_ref, column, row, product_ref):
    zero = jnp.zeros((HALF, 128), BF16)

    def pair(k0, k1):
        lhs = jnp.concatenate([pt_ref[column(k0, row)], pt_ref[column(k1, row)]], axis=1)
        weights = jnp.concatenate([
            jnp.concatenate([x_ref[row, k0], zero], axis=1),
            jnp.concatenate([zero, x_ref[row, k1]], axis=1)], axis=0)
        return lax.dot_general(lhs, weights, NT, preferred_element_type=F32).astype(BF16)

    for group in range(QUADS):
        k = [min(group * 4 + n, SLOTS - 1) for n in range(4)]
        both = jnp.concatenate([pair(k[0], k[1]), pair(k[2], k[3])], axis=1)
        rows = slice(group * HALF, (group + 1) * HALF)
        product_ref[0, rows, :] = both[0:HALF]
        product_ref[1, rows, :] = both[HALF:BLOCK]


def accumulate(pi_ref, place, row, product_ref, accs):
    block = iota((BLOCK, 128), 1) // 32
    even, odd = pi_ref[row, 0], pi_ref[row, 1]
    zero = jnp.zeros_like(even)
    weights = jnp.concatenate([
        jnp.concatenate([jnp.where(block == n, even, zero), jnp.where(block == n, odd, zero)], axis=1)
        for n in range(4)], axis=0)
    lhs = jnp.concatenate([product_ref[0], product_ref[1]], axis=1)
    triple = lax.dot_general(lhs, weights, NT, preferred_element_type=F32)
    for k in range(SLOTS):
        group, n = divmod(k, 4)
        at = place(k, row)
        lanes = slice((n % 2) * BLOCK, (n % 2 + 1) * BLOCK)
        value = triple[group * HALF:(group + 1) * HALF, n * BLOCK:(n + 1) * BLOCK]
        acc_ref = accs[n % 2]
        acc_ref[at, :, lanes] = acc_ref[at, :, lanes] + value


def finish(accs, fold_ref, out_ref, tile):
    side = iota((HALF, 128), 1) < BLOCK
    stacked = jnp.concatenate([jnp.where(side, accs[0][tile + s], accs[1][tile + s]) for s in range(4)], axis=0)
    head = stacked.astype(BF16)
    tail = (stacked - head.astype(F32)).astype(BF16)
    turned = lax.dot_general(
        fold_ref[...], jnp.concatenate([head, tail], axis=1), NT, preferred_element_type=F32)
    p = [turned[r * 16:(r + 1) * 16] for r in range(4)]
    lane = iota((16, 128), 1)
    low, even = lane < 64, lane % 64 < 32
    u = [jnp.where(low, p[0], pltpu.roll(p[2], 64, 1)), jnp.where(low, p[1], pltpu.roll(p[3], 64, 1)),
         jnp.where(low, pltpu.roll(p[0], 64, 1), p[2]), jnp.where(low, pltpu.roll(p[1], 64, 1), p[3])]
    for s in range(4):
        a, b = u[s // 2 * 2], u[s // 2 * 2 + 1]
        value = jnp.where(even, a, pltpu.roll(b, 32, 1)) if s % 2 == 0 else jnp.where(even, pltpu.roll(a, 96, 1), b)
        out_ref[pl.ds(pl.multiple_of((tile + s) * 16, 16), 16), :] = value


def exchange_kernel(blocks_hbm, own_hbm, x_hbm, left_hbm, right_hbm, other_hbm,
                    blocks_ref, x_ref, perm_ref, in_sems, out_sems, send_sems, recv_sems):
    r, o, c = lax.axis_index("rows"), lax.axis_index("owners"), lax.axis_index("rep")
    rows, owners = lax.axis_size("rows"), lax.axis_size("owners")
    groups = rows * owners
    group = r * owners + o
    after, before = (group + 1) % groups, (group + groups - 1) % groups
    targets = [(after // owners, after % owners, c), (before // owners, before % owners, c), (r, o, 1 - c)]
    barrier = pltpu.get_barrier_semaphore()
    for target in targets:
        pl.semaphore_signal(barrier, inc=1, device_id=target, device_id_type=pl.DeviceIdType.MESH)

    def pieces(part):
        return pl.ds(pl.multiple_of(part // 3 * TILE, TILE), TILE), pl.ds(part % 3 * PART, PART)

    def fetch(part):
        rows_at, slots_at = pieces(part)
        return pltpu.make_async_copy(
            blocks_hbm.at[slots_at, rows_at, :], blocks_ref.at[slots_at, rows_at, :], in_sems.at[part])

    def keep(part):
        rows_at, slots_at = pieces(part)
        return pltpu.make_async_copy(x_ref.at[rows_at, slots_at], x_hbm.at[rows_at, slots_at], out_sems.at[part])

    for part in range(EARLY):
        fetch(part).start()

    def turn(part, _):
        fetch(part).wait()
        for q in range(PART):
            relayout(blocks_ref, x_ref, perm_ref, part // 3, part % 3 * PART + q)
        keep(part).start()
        return 0

    pl.semaphore_wait(barrier, 3)
    copies = []
    for n, (target, landing) in enumerate(zip(targets, (left_hbm, right_hbm, other_hbm))):
        copies.append(pltpu.make_async_remote_copy(
            src_ref=own_hbm, dst_ref=landing, send_sem=send_sems.at[n], recv_sem=recv_sems.at[n],
            device_id=target, device_id_type=pl.DeviceIdType.MESH))
    for copy in copies:
        copy.start()
    for part in range(EARLY, 9):
        fetch(part).start()
    row, lane = iota((256, 256), 0), iota((256, 256), 1)
    perm_ref[...] = one_hot((row // 16 == lane % 16) & (row % 16 == lane // 16))
    lax.fori_loop(0, 9, turn, 0)
    for part in range(9):
        keep(part).wait()
    for copy in copies:
        copy.wait()


def exchange(blocks, own):
    anywhere = pl.BlockSpec(memory_space=pl.ANY)
    panel = jax.ShapeDtypeStruct((ROWS, 2048), BF16)
    return pl.pallas_call(
        exchange_kernel,
        out_shape=(jax.ShapeDtypeStruct((ROWS, SLOTS, HALF, 128), BF16), panel, panel, panel),
        in_specs=[anywhere, anywhere],
        out_specs=(anywhere, anywhere, anywhere, anywhere),
        scratch_shapes=[
            pltpu.VMEM((SLOTS, ROWS, BLOCK * BLOCK), BF16),
            pltpu.VMEM((ROWS, SLOTS, HALF, 128), BF16),
            pltpu.VMEM((256, 256), BF16),
            pltpu.SemaphoreType.DMA((9,)),
            pltpu.SemaphoreType.DMA((9,)),
            pltpu.SemaphoreType.DMA((3,)),
            pltpu.SemaphoreType.DMA((3,)),
        ],
        compiler_params=pltpu.CompilerParams(
            vmem_limit_bytes=60 << 20, collective_id=0, has_side_effects=True),
        name="turn_blocks",
    )(blocks, own)


def kernel(cols_ref, slots_ref, agg_ref, x_hbm, left_ref, own_ref, right_ref, other_ref, out_hbm,
           x_ref, pt_ref, pi_ref, acc_ref, second_ref, spread_ref, order_ref, fold_ref, out_ref,
           *rest):
    product_refs, (in_sems, out_sems) = rest[:STEP], rest[STEP:]
    accs = (acc_ref, second_ref)
    group = lax.axis_index("rows") * lax.axis_size("owners") + lax.axis_index("owners")
    first_row, first_coarse = group * ROWS, group * AGGS

    def fetch(part):
        rows = pl.ds(pl.multiple_of(part * FETCH, FETCH), FETCH)
        return pltpu.make_async_copy(x_hbm.at[rows], x_ref.at[rows], in_sems.at[part])

    for part in range(ROWS // FETCH):
        fetch(part).start()

    prepare((left_ref, own_ref, right_ref, other_ref), lax.axis_index("rep"), spread_ref, order_ref, pt_ref, pi_ref)
    row, lane = iota((BLOCK, 256), 0), iota((BLOCK, 256), 1)
    fold_ref[...] = one_hot(4 * (row % 16) + row // 16 == lane % 64)

    @pl.loop(0, AGGS)
    def _(t):
        for s in range(CSLOTS):
            acc_ref[t * CSLOTS + s, :, 0:BLOCK] = jnp.zeros((HALF, BLOCK), F32)
            second_ref[t * CSLOTS + s, :, BLOCK:128] = jnp.zeros((HALF, BLOCK), F32)

    fetch(0).wait()

    def column(k, row):
        near = cols_ref[k, row] - first_row + ROWS
        near = jnp.where(near < 0, near + FINE, near)
        return jnp.where(near >= FINE, near - FINE, near)

    def place(k, row):
        return (agg_ref[row] - first_coarse) * CSLOTS + slots_ref[k, row]

    products(x_ref, pt_ref, column, 0, product_refs[0])

    @pl.loop(0, ROWS // STEP)
    def _(block):
        @pl.when(block < ROWS // FETCH - 1)
        def _():
            fetch(block + 1).wait()

        for n in range(STEP):
            row = block * STEP + n
            products(x_ref, pt_ref, column, jnp.minimum(row + 1, ROWS - 1), product_refs[(n + 1) % STEP])
            accumulate(pi_ref, place, row, product_refs[n], accs)

    def send(chunk):
        rows = pl.ds(pl.multiple_of(chunk * (CHUNK * 64), CHUNK * 64), CHUNK * 64)
        return pltpu.make_async_copy(out_ref.at[rows, :], out_hbm.at[rows, :], out_sems.at[chunk])

    @pl.loop(0, CHUNKS)
    def _(chunk):
        for g in range(CHUNK):
            finish(accs, fold_ref, out_ref, (chunk * CHUNK + g) * 4)
        send(chunk).start()

    @pl.loop(0, CHUNKS)
    def _(chunk):
        send(chunk).wait()


def combine(cols, slots, agg, x, left, own, right, other):
    vmem = pl.BlockSpec(memory_space=pltpu.VMEM)
    smem = pl.BlockSpec(memory_space=pltpu.SMEM)
    anywhere = pl.BlockSpec(memory_space=pl.ANY)
    return pl.pallas_call(
        kernel,
        out_shape=jax.ShapeDtypeStruct((AGGS * CSLOTS * 16, 128), F32),
        in_specs=[smem, smem, smem, anywhere, vmem, vmem, vmem, vmem],
        out_specs=anywhere,
        scratch_shapes=[
            pltpu.VMEM((ROWS, SLOTS, HALF, 128), BF16),
            pltpu.VMEM((3 * ROWS, BLOCK, 128), BF16),
            pltpu.VMEM((ROWS, 2, BLOCK, 128), BF16),
            pltpu.VMEM((AGGS * CSLOTS, HALF, 128), F32),
            pltpu.VMEM((AGGS * CSLOTS, HALF, 128), F32),
            pltpu.VMEM((512, 1024), BF16),
            pltpu.VMEM((512, 2048), BF16),
            pltpu.VMEM((BLOCK, 256), BF16),
            pltpu.VMEM((AGGS * CSLOTS * 16, 128), F32),
            *[pltpu.VMEM((2, QUADS * HALF, 128), BF16)] * STEP,
            pltpu.SemaphoreType.DMA((ROWS // FETCH,)),
            pltpu.SemaphoreType.DMA((CHUNKS,)),
        ],
        compiler_params=pltpu.CompilerParams(vmem_limit_bytes=60 << 20),
        name="galerkin",
    )(cols, slots, agg, x, left, own, right, other)


def shards(blocks, panels, columns, aggregate, coarse_slots):
    own = panels.reshape(ROWS, 2048)
    x, left, right, other = exchange(jnp.transpose(blocks, (1, 0, 2)), own)
    out = combine(columns.T, coarse_slots.T, aggregate, x, left, own, right, other)
    return out.reshape(AGGS, CSLOTS, 1, 2048)


def solution(mesh):
    return jax.shard_map(
        shards,
        mesh=mesh,
        in_specs=(
            P(("rows", "owners"), None, None),
            P(("rows", "owners"), "rep", None),
            P(("rows", "owners"), None),
            P(("rows", "owners")),
            P(("rows", "owners"), None),
        ),
        out_specs=P(("rows", "owners"), None, "rep", None),
        check_vma=False,
    )
```

```python
import jax
import jax.numpy as jnp
from jax import lax
from jax.experimental import pallas as pl
from jax.experimental.pallas import tpu as pltpu
from jax.sharding import PartitionSpec as P

BLOCK = 64
HALF = 32
SLOTS = 27
ROWS = 48
AGGS = 16
CSLOTS = 33
TILE = 16
TILES = ROWS // TILE
PART = 9
EARLY = 9
STEP = 8
FINE = 6144
QUADS = 7
CHUNK = 33
CHUNKS = AGGS * CSLOTS // 4 // CHUNK
F32 = jnp.float32
BF16 = jnp.bfloat16
NT = (((1,), (1,)), ((), ()))


def iota(shape, dim):
    return lax.broadcasted_iota(jnp.int32, shape, dim)


def one_hot(mask):
    return jnp.where(mask, 1.0, 0.0).astype(F32).astype(BF16)


def prepare(refs, rep, spread_ref, order_ref, pt_ref, pi_ref):
    def table(ref, width, shift, place_of):
        row, lane = iota((128, 8 * width), 0), iota((128, 8 * width), 1)
        ahead = place_of(lane & (width - 1)) - ((row >> 3) << 2)
        ahead = jnp.where((row & 7) == (lane >> shift), ahead, -1)
        for r in range(4):
            ref[r * 128:(r + 1) * 128, :] = one_hot(ahead == r)

    table(spread_ref, 128, 7, lambda p: p & 63)
    table(order_ref, 256, 8, lambda p: (((p >> 4) & 1) << 5) + ((p & 15) << 1) + (p >> 7))

    left, own, right, other = refs

    def transposed(ref):
        parts = []
        for q in range(TILES):
            rows16 = ref[q * TILE:(q + 1) * TILE, :].astype(F32)
            for half in range(2):
                rows8 = rows16[half * 8:half * 8 + 8, :]
                stacked = jnp.concatenate([rows8[:, u * 128:(u + 1) * 128] for u in range(16)], axis=0)
                turned = stacked.T.astype(BF16)
                parts.append(jnp.concatenate([turned[r * 32:(r + 1) * 32, :] for r in range(4)], axis=1))
        return jnp.concatenate(parts, axis=0)

    def put(result, width, store):
        result = result.astype(BF16)
        for group in range(6):
            for j in range(8):
                store(group * 8 + j, result[group * 32:(group + 1) * 32, j * width:(j + 1) * width])

    first = iota((HALF, 128), 1) < 64
    for base, ref in ((0, left), (ROWS, own), (2 * ROWS, right)):
        lhs = transposed(ref)

        def store_pt(j, value, base=base):
            zero = jnp.zeros_like(value)
            pt_ref[base + j, 0:HALF, :] = jnp.where(first, value, zero)
            pt_ref[base + j, HALF:BLOCK, :] = jnp.where(first, zero, value)

        put(jnp.dot(lhs, spread_ref[...], preferred_element_type=F32), 128, store_pt)
    for ref, half in ((own, rep), (other, 1 - rep)):
        lhs = transposed(ref)
        start = pl.multiple_of(half * HALF, HALF)

        def store_pi(i, value, start=start):
            pi_ref[i, 0, pl.ds(start, HALF), :] = value[:, 0:128]
            pi_ref[i, 1, pl.ds(start, HALF), :] = value[:, 128:256]

        put(jnp.dot(lhs, order_ref[...], preferred_element_type=F32), 256, store_pi)


def relayout(blocks_ref, x_ref, perm_ref, tile, k):
    native = blocks_ref[k, pl.ds(pl.multiple_of(tile * TILE, TILE), TILE), :]
    halves = []
    for high in range(2):
        halves.append(jnp.concatenate(
            [native[:, (high * 16 + t) * 128:(high * 16 + t + 1) * 128] for t in range(16)], axis=0))
    rhs = jnp.concatenate(halves, axis=1)
    result = jnp.dot(perm_ref[...], rhs, preferred_element_type=F32).astype(BF16)
    for i in range(TILE):
        x_ref[tile * TILE + i, k, 0:16, :] = result[i * 16:(i + 1) * 16, 0:128]
        x_ref[tile * TILE + i, k, 16:32, :] = result[i * 16:(i + 1) * 16, 128:256]


def products(x_ref, pt_ref, column, row, product_ref):
    zero = jnp.zeros((HALF, 128), BF16)

    def pair(k0, k1):
        lhs = jnp.concatenate([pt_ref[column(k0, row)], pt_ref[column(k1, row)]], axis=1)
        weights = jnp.concatenate([
            jnp.concatenate([x_ref[row, k0], zero], axis=1),
            jnp.concatenate([zero, x_ref[row, k1]], axis=1)], axis=0)
        return lax.dot_general(lhs, weights, NT, preferred_element_type=F32).astype(BF16)

    for group in range(QUADS):
        k = [min(group * 4 + n, SLOTS - 1) for n in range(4)]
        both = jnp.concatenate([pair(k[0], k[1]), pair(k[2], k[3])], axis=1)
        rows = slice(group * HALF, (group + 1) * HALF)
        product_ref[0, rows, :] = both[0:HALF]
        product_ref[1, rows, :] = both[HALF:BLOCK]


def accumulate(pi_ref, place, row, product_ref, accs):
    block = iota((BLOCK, 128), 1) // 32
    even, odd = pi_ref[row, 0], pi_ref[row, 1]
    zero = jnp.zeros_like(even)
    weights = jnp.concatenate([
        jnp.concatenate([jnp.where(block == n, even, zero), jnp.where(block == n, odd, zero)], axis=1)
        for n in range(4)], axis=0)
    lhs = jnp.concatenate([product_ref[0], product_ref[1]], axis=1)
    triple = lax.dot_general(lhs, weights, NT, preferred_element_type=F32)
    for k in range(SLOTS):
        group, n = divmod(k, 4)
        at = place(k, row)
        lanes = slice((n % 2) * BLOCK, (n % 2 + 1) * BLOCK)
        value = triple[group * HALF:(group + 1) * HALF, n * BLOCK:(n + 1) * BLOCK]
        acc_ref = accs[n % 2]
        acc_ref[at, :, lanes] = acc_ref[at, :, lanes] + value


def finish(accs, fold_ref, out_ref, tile):
    side = iota((HALF, 128), 1) < BLOCK
    stacked = jnp.concatenate([jnp.where(side, accs[0][tile + s], accs[1][tile + s]) for s in range(4)], axis=0)
    head = stacked.astype(BF16)
    tail = (stacked - head.astype(F32)).astype(BF16)
    turned = lax.dot_general(
        fold_ref[...], jnp.concatenate([head, tail], axis=1), NT, preferred_element_type=F32)
    p = [turned[r * 16:(r + 1) * 16] for r in range(4)]
    lane = iota((16, 128), 1)
    low, even = lane < 64, lane % 64 < 32
    u = [jnp.where(low, p[0], pltpu.roll(p[2], 64, 1)), jnp.where(low, p[1], pltpu.roll(p[3], 64, 1)),
         jnp.where(low, pltpu.roll(p[0], 64, 1), p[2]), jnp.where(low, pltpu.roll(p[1], 64, 1), p[3])]
    for s in range(4):
        a, b = u[s // 2 * 2], u[s // 2 * 2 + 1]
        value = jnp.where(even, a, pltpu.roll(b, 32, 1)) if s % 2 == 0 else jnp.where(even, pltpu.roll(a, 96, 1), b)
        out_ref[pl.ds(pl.multiple_of((tile + s) * 16, 16), 16), :] = value


def exchange_kernel(blocks_hbm, own_hbm, x_ref, left_hbm, right_hbm, other_hbm,
                    blocks_ref, perm_ref, in_sems, send_sems, recv_sems):
    r, o, c = lax.axis_index("rows"), lax.axis_index("owners"), lax.axis_index("rep")
    rows, owners = lax.axis_size("rows"), lax.axis_size("owners")
    groups = rows * owners
    group = r * owners + o
    after, before = (group + 1) % groups, (group + groups - 1) % groups
    targets = [(after // owners, after % owners, c), (before // owners, before % owners, c), (r, o, 1 - c)]
    barrier = pltpu.get_barrier_semaphore()
    for target in targets:
        pl.semaphore_signal(barrier, inc=1, device_id=target, device_id_type=pl.DeviceIdType.MESH)

    def pieces(part):
        return pl.ds(pl.multiple_of(part // 3 * TILE, TILE), TILE), pl.ds(part % 3 * PART, PART)

    def fetch(part):
        rows_at, slots_at = pieces(part)
        return pltpu.make_async_copy(
            blocks_hbm.at[slots_at, rows_at, :], blocks_ref.at[slots_at, rows_at, :], in_sems.at[part])

    for part in range(EARLY):
        fetch(part).start()

    def turn(part, _):
        fetch(part).wait()
        for q in range(PART):
            relayout(blocks_ref, x_ref, perm_ref, part // 3, part % 3 * PART + q)
        return 0

    pl.semaphore_wait(barrier, 3)
    copies = []
    for n, (target, landing) in enumerate(zip(targets, (left_hbm, right_hbm, other_hbm))):
        copies.append(pltpu.make_async_remote_copy(
            src_ref=own_hbm, dst_ref=landing, send_sem=send_sems.at[n], recv_sem=recv_sems.at[n],
            device_id=target, device_id_type=pl.DeviceIdType.MESH))
    for copy in copies:
        copy.start()
    for part in range(EARLY, 9):
        fetch(part).start()
    row, lane = iota((256, 256), 0), iota((256, 256), 1)
    perm_ref[...] = one_hot((row // 16 == lane % 16) & (row % 16 == lane // 16))
    lax.fori_loop(0, 9, turn, 0)
    for copy in copies:
        copy.wait()


def exchange(blocks, own):
    anywhere = pl.BlockSpec(memory_space=pl.ANY)
    panel = jax.ShapeDtypeStruct((ROWS, 2048), BF16)
    return pl.pallas_call(
        exchange_kernel,
        out_shape=(pltpu.VMEM((ROWS, SLOTS, HALF, 128), BF16), panel, panel, panel),
        in_specs=[anywhere, anywhere],
        out_specs=(pl.BlockSpec(memory_space=pltpu.VMEM), anywhere, anywhere, anywhere),
        scratch_shapes=[
            pltpu.VMEM((SLOTS, ROWS, BLOCK * BLOCK), BF16),
            pltpu.VMEM((256, 256), BF16),
            pltpu.SemaphoreType.DMA((9,)),
            pltpu.SemaphoreType.DMA((3,)),
            pltpu.SemaphoreType.DMA((3,)),
        ],
        compiler_params=pltpu.CompilerParams(
            vmem_limit_bytes=48 << 20, collective_id=0, has_side_effects=True),
        name="turn_blocks",
    )(blocks, own)


def kernel(cols_ref, slots_ref, agg_ref, x_ref, left_ref, own_ref, right_ref, other_ref, out_hbm,
           pt_ref, pi_ref, acc_ref, second_ref, spread_ref, order_ref, fold_ref, out_ref,
           *rest):
    product_refs, (out_sems,) = rest[:STEP], rest[STEP:]
    accs = (acc_ref, second_ref)
    group = lax.axis_index("rows") * lax.axis_size("owners") + lax.axis_index("owners")
    first_row, first_coarse = group * ROWS, group * AGGS

    prepare((left_ref, own_ref, right_ref, other_ref), lax.axis_index("rep"), spread_ref, order_ref, pt_ref, pi_ref)
    row, lane = iota((BLOCK, 256), 0), iota((BLOCK, 256), 1)
    fold_ref[...] = one_hot(4 * (row % 16) + row // 16 == lane % 64)

    @pl.loop(0, AGGS)
    def _(t):
        for s in range(CSLOTS):
            acc_ref[t * CSLOTS + s, :, 0:BLOCK] = jnp.zeros((HALF, BLOCK), F32)
            second_ref[t * CSLOTS + s, :, BLOCK:128] = jnp.zeros((HALF, BLOCK), F32)

    def column(k, row):
        near = cols_ref[k, row] - first_row + ROWS
        near = jnp.where(near < 0, near + FINE, near)
        return jnp.where(near >= FINE, near - FINE, near)

    def place(k, row):
        return (agg_ref[row] - first_coarse) * CSLOTS + slots_ref[k, row]

    products(x_ref, pt_ref, column, 0, product_refs[0])

    @pl.loop(0, ROWS // STEP)
    def _(block):
        for n in range(STEP):
            row = block * STEP + n
            products(x_ref, pt_ref, column, jnp.minimum(row + 1, ROWS - 1), product_refs[(n + 1) % STEP])
            accumulate(pi_ref, place, row, product_refs[n], accs)

    def send(chunk):
        rows = pl.ds(pl.multiple_of(chunk * (CHUNK * 64), CHUNK * 64), CHUNK * 64)
        return pltpu.make_async_copy(out_ref.at[rows, :], out_hbm.at[rows, :], out_sems.at[chunk])

    @pl.loop(0, CHUNKS)
    def _(chunk):
        for g in range(CHUNK):
            finish(accs, fold_ref, out_ref, (chunk * CHUNK + g) * 4)
        send(chunk).start()

    @pl.loop(0, CHUNKS)
    def _(chunk):
        send(chunk).wait()


def combine(cols, slots, agg, x, left, own, right, other):
    vmem = pl.BlockSpec(memory_space=pltpu.VMEM)
    smem = pl.BlockSpec(memory_space=pltpu.SMEM)
    anywhere = pl.BlockSpec(memory_space=pl.ANY)
    return pl.pallas_call(
        kernel,
        out_shape=jax.ShapeDtypeStruct((AGGS * CSLOTS * 16, 128), F32),
        in_specs=[smem, smem, smem, vmem, vmem, vmem, vmem, vmem],
        out_specs=anywhere,
        scratch_shapes=[
            pltpu.VMEM((3 * ROWS, BLOCK, 128), BF16),
            pltpu.VMEM((ROWS, 2, BLOCK, 128), BF16),
            pltpu.VMEM((AGGS * CSLOTS, HALF, 128), F32),
            pltpu.VMEM((AGGS * CSLOTS, HALF, 128), F32),
            pltpu.VMEM((512, 1024), BF16),
            pltpu.VMEM((512, 2048), BF16),
            pltpu.VMEM((BLOCK, 256), BF16),
            pltpu.VMEM((AGGS * CSLOTS * 16, 128), F32),
            *[pltpu.VMEM((2, QUADS * HALF, 128), BF16)] * STEP,
            pltpu.SemaphoreType.DMA((CHUNKS,)),
        ],
        compiler_params=pltpu.CompilerParams(vmem_limit_bytes=36 << 20),
        name="galerkin",
    )(cols, slots, agg, x, left, own, right, other)


def shards(blocks, panels, columns, aggregate, coarse_slots):
    own = panels.reshape(ROWS, 2048)
    x, left, right, other = exchange(jnp.transpose(blocks, (1, 0, 2)), own)
    out = combine(columns.T, coarse_slots.T, aggregate, x, left, own, right, other)
    return out.reshape(AGGS, CSLOTS, 1, 2048)


def solution(mesh):
    return jax.shard_map(
        shards,
        mesh=mesh,
        in_specs=(
            P(("rows", "owners"), None, None),
            P(("rows", "owners"), "rep", None),
            P(("rows", "owners"), None),
            P(("rows", "owners")),
            P(("rows", "owners"), None),
        ),
        out_specs=P(("rows", "owners"), None, "rep", None),
        check_vma=False,
    )
```

```python
import jax
import jax.numpy as jnp
from jax import lax
from jax.experimental import pallas as pl
from jax.experimental.pallas import tpu as pltpu
from jax.sharding import PartitionSpec as P

BLOCK = 64
HALF = 32
SLOTS = 27
ROWS = 48
AGGS = 16
CSLOTS = 33
TILE = 16
TILES = ROWS // TILE
PART = 9
EARLY = 9
STEP = 8
FINE = 6144
QUADS = 7
CHUNK = 33
CHUNKS = AGGS * CSLOTS // 4 // CHUNK
F32 = jnp.float32
BF16 = jnp.bfloat16
NT = (((1,), (1,)), ((), ()))


def iota(shape, dim):
    return lax.broadcasted_iota(jnp.int32, shape, dim)


def one_hot(mask):
    return jnp.where(mask, 1.0, 0.0).astype(F32).astype(BF16)


def prepare(refs, rep, spread_ref, order_ref, pt_ref, pi_ref):
    def table(ref, width, shift, place_of):
        row, lane = iota((128, 8 * width), 0), iota((128, 8 * width), 1)
        ahead = place_of(lane & (width - 1)) - ((row >> 3) << 2)
        ahead = jnp.where((row & 7) == (lane >> shift), ahead, -1)
        for r in range(4):
            ref[r * 128:(r + 1) * 128, :] = one_hot(ahead == r)

    table(spread_ref, 128, 7, lambda p: p & 63)
    table(order_ref, 256, 8, lambda p: (((p >> 4) & 1) << 5) + ((p & 15) << 1) + (p >> 7))

    left, own, right, other = refs

    def transposed(ref):
        parts = []
        for q in range(TILES):
            rows16 = ref[q * TILE:(q + 1) * TILE, :].astype(F32)
            for half in range(2):
                rows8 = rows16[half * 8:half * 8 + 8, :]
                stacked = jnp.concatenate([rows8[:, u * 128:(u + 1) * 128] for u in range(16)], axis=0)
                turned = stacked.T.astype(BF16)
                parts.append(jnp.concatenate([turned[r * 32:(r + 1) * 32, :] for r in range(4)], axis=1))
        return jnp.concatenate(parts, axis=0)

    def put(result, width, store):
        result = result.astype(BF16)
        for group in range(6):
            for j in range(8):
                store(group * 8 + j, result[group * 32:(group + 1) * 32, j * width:(j + 1) * width])

    first = iota((HALF, 128), 1) < 64
    for base, ref in ((0, left), (ROWS, own), (2 * ROWS, right)):
        lhs = transposed(ref)

        def store_pt(j, value, base=base):
            zero = jnp.zeros_like(value)
            pt_ref[base + j, 0:HALF, :] = jnp.where(first, value, zero)
            pt_ref[base + j, HALF:BLOCK, :] = jnp.where(first, zero, value)

        put(jnp.dot(lhs, spread_ref[...], preferred_element_type=F32), 128, store_pt)
    for ref, half in ((own, rep), (other, 1 - rep)):
        lhs = transposed(ref)
        start = pl.multiple_of(half * HALF, HALF)

        def store_pi(i, value, start=start):
            pi_ref[i, 0, pl.ds(start, HALF), :] = value[:, 0:128]
            pi_ref[i, 1, pl.ds(start, HALF), :] = value[:, 128:256]

        put(jnp.dot(lhs, order_ref[...], preferred_element_type=F32), 256, store_pi)


def relayout(blocks_ref, x_ref, perm_ref, tile, k):
    native = blocks_ref[k, pl.ds(pl.multiple_of(tile * TILE, TILE), TILE), :]
    halves = []
    for high in range(2):
        halves.append(jnp.concatenate(
            [native[:, (high * 16 + t) * 128:(high * 16 + t + 1) * 128] for t in range(16)], axis=0))
    rhs = jnp.concatenate(halves, axis=1)
    result = jnp.dot(perm_ref[...], rhs, preferred_element_type=F32).astype(BF16)
    for i in range(TILE):
        x_ref[tile * TILE + i, k, 0:16, :] = result[i * 16:(i + 1) * 16, 0:128]
        x_ref[tile * TILE + i, k, 16:32, :] = result[i * 16:(i + 1) * 16, 128:256]


def products(x_ref, pt_ref, column, row, product_ref):
    zero = jnp.zeros((HALF, 128), BF16)

    def pair(k0, k1):
        lhs = jnp.concatenate([pt_ref[column(k0, row)], pt_ref[column(k1, row)]], axis=1)
        weights = jnp.concatenate([
            jnp.concatenate([x_ref[row, k0], zero], axis=1),
            jnp.concatenate([zero, x_ref[row, k1]], axis=1)], axis=0)
        return lax.dot_general(lhs, weights, NT, preferred_element_type=F32).astype(BF16)

    for group in range(QUADS):
        k = [min(group * 4 + n, SLOTS - 1) for n in range(4)]
        both = jnp.concatenate([pair(k[0], k[1]), pair(k[2], k[3])], axis=1)
        rows = slice(group * HALF, (group + 1) * HALF)
        product_ref[0, rows, :] = both[0:HALF]
        product_ref[1, rows, :] = both[HALF:BLOCK]


def accumulate(pi_ref, place, row, product_ref, accs):
    block = iota((BLOCK, 128), 1) // 32
    even, odd = pi_ref[row, 0], pi_ref[row, 1]
    zero = jnp.zeros_like(even)
    weights = jnp.concatenate([
        jnp.concatenate([jnp.where(block == n, even, zero), jnp.where(block == n, odd, zero)], axis=1)
        for n in range(4)], axis=0)
    lhs = jnp.concatenate([product_ref[0], product_ref[1]], axis=1)
    triple = lax.dot_general(lhs, weights, NT, preferred_element_type=F32)
    for k in range(SLOTS):
        group, n = divmod(k, 4)
        at = place(k, row)
        lanes = slice((n % 2) * BLOCK, (n % 2 + 1) * BLOCK)
        value = triple[group * HALF:(group + 1) * HALF, n * BLOCK:(n + 1) * BLOCK]
        acc_ref = accs[n % 2]
        acc_ref[at, :, lanes] = acc_ref[at, :, lanes] + value


def finish(accs, fold_ref, out_ref, tile):
    side = iota((HALF, 128), 1) < BLOCK
    stacked = jnp.concatenate([jnp.where(side, accs[0][tile + s], accs[1][tile + s]) for s in range(4)], axis=0)
    head = stacked.astype(BF16)
    tail = (stacked - head.astype(F32)).astype(BF16)
    turned = lax.dot_general(
        fold_ref[...], jnp.concatenate([head, tail], axis=1), NT, preferred_element_type=F32)
    p = [turned[r * 16:(r + 1) * 16] for r in range(4)]
    lane = iota((16, 128), 1)
    low, even = lane < 64, lane % 64 < 32
    u = [jnp.where(low, p[0], pltpu.roll(p[2], 64, 1)), jnp.where(low, p[1], pltpu.roll(p[3], 64, 1)),
         jnp.where(low, pltpu.roll(p[0], 64, 1), p[2]), jnp.where(low, pltpu.roll(p[1], 64, 1), p[3])]
    for s in range(4):
        a, b = u[s // 2 * 2], u[s // 2 * 2 + 1]
        value = jnp.where(even, a, pltpu.roll(b, 32, 1)) if s % 2 == 0 else jnp.where(even, pltpu.roll(a, 96, 1), b)
        out_ref[pl.ds(pl.multiple_of((tile + s) * 16, 16), 16), :] = value


def exchange_kernel(blocks_hbm, own_hbm, x_ref, left_hbm, right_hbm, other_hbm,
                    blocks_ref, perm_ref, in_sems, send_sems, recv_sems):
    r, o, c = lax.axis_index("rows"), lax.axis_index("owners"), lax.axis_index("rep")
    rows, owners = lax.axis_size("rows"), lax.axis_size("owners")
    groups = rows * owners
    group = r * owners + o
    after, before = (group + 1) % groups, (group + groups - 1) % groups
    targets = [(after // owners, after % owners, c), (before // owners, before % owners, c), (r, o, 1 - c)]
    barrier = pltpu.get_barrier_semaphore()
    for target in targets:
        pl.semaphore_signal(barrier, inc=1, device_id=target, device_id_type=pl.DeviceIdType.MESH)

    def pieces(part):
        return pl.ds(pl.multiple_of(part // 3 * TILE, TILE), TILE), pl.ds(part % 3 * PART, PART)

    def fetch(part):
        rows_at, slots_at = pieces(part)
        return pltpu.make_async_copy(
            blocks_hbm.at[slots_at, rows_at, :], blocks_ref.at[slots_at, rows_at, :], in_sems.at[part])

    for part in range(EARLY):
        fetch(part).start()

    def turn(part, _):
        fetch(part).wait()
        for q in range(PART):
            relayout(blocks_ref, x_ref, perm_ref, part // 3, part % 3 * PART + q)
        return 0

    pl.semaphore_wait(barrier, 3)
    copies = []
    for n, (target, landing) in enumerate(zip(targets, (left_hbm, right_hbm, other_hbm))):
        copies.append(pltpu.make_async_remote_copy(
            src_ref=own_hbm, dst_ref=landing, send_sem=send_sems.at[n], recv_sem=recv_sems.at[n],
            device_id=target, device_id_type=pl.DeviceIdType.MESH))
    for copy in copies:
        copy.start()
    for part in range(EARLY, 9):
        fetch(part).start()
    row, lane = iota((256, 256), 0), iota((256, 256), 1)
    perm_ref[...] = one_hot((row // 16 == lane % 16) & (row % 16 == lane // 16))
    lax.fori_loop(0, 9, turn, 0)
    for copy in copies:
        copy.wait()


def exchange(blocks, own):
    anywhere = pl.BlockSpec(memory_space=pl.ANY)
    panel = pltpu.VMEM((ROWS, 2048), BF16)
    return pl.pallas_call(
        exchange_kernel,
        out_shape=(pltpu.VMEM((ROWS, SLOTS, HALF, 128), BF16), panel, panel, panel),
        in_specs=[anywhere, anywhere],
        out_specs=(pl.BlockSpec(memory_space=pltpu.VMEM),) * 4,
        scratch_shapes=[
            pltpu.VMEM((SLOTS, ROWS, BLOCK * BLOCK), BF16),
            pltpu.VMEM((256, 256), BF16),
            pltpu.SemaphoreType.DMA((9,)),
            pltpu.SemaphoreType.DMA((3,)),
            pltpu.SemaphoreType.DMA((3,)),
        ],
        compiler_params=pltpu.CompilerParams(
            vmem_limit_bytes=48 << 20, collective_id=0, has_side_effects=True),
        name="turn_blocks",
    )(blocks, own)


def kernel(cols_ref, slots_ref, agg_ref, x_ref, left_ref, own_ref, right_ref, other_ref, out_hbm,
           pt_ref, pi_ref, acc_ref, second_ref, spread_ref, order_ref, fold_ref, out_ref,
           *rest):
    product_refs, (out_sems,) = rest[:STEP], rest[STEP:]
    accs = (acc_ref, second_ref)
    group = lax.axis_index("rows") * lax.axis_size("owners") + lax.axis_index("owners")
    first_row, first_coarse = group * ROWS, group * AGGS

    prepare((left_ref, own_ref, right_ref, other_ref), lax.axis_index("rep"), spread_ref, order_ref, pt_ref, pi_ref)
    row, lane = iota((BLOCK, 256), 0), iota((BLOCK, 256), 1)
    fold_ref[...] = one_hot(4 * (row % 16) + row // 16 == lane % 64)

    @pl.loop(0, AGGS)
    def _(t):
        for s in range(CSLOTS):
            acc_ref[t * CSLOTS + s, :, 0:BLOCK] = jnp.zeros((HALF, BLOCK), F32)
            second_ref[t * CSLOTS + s, :, BLOCK:128] = jnp.zeros((HALF, BLOCK), F32)

    def column(k, row):
        near = cols_ref[k, row] - first_row + ROWS
        near = jnp.where(near < 0, near + FINE, near)
        return jnp.where(near >= FINE, near - FINE, near)

    def place(k, row):
        return (agg_ref[row] - first_coarse) * CSLOTS + slots_ref[k, row]

    products(x_ref, pt_ref, column, 0, product_refs[0])

    @pl.loop(0, ROWS // STEP)
    def _(block):
        for n in range(STEP):
            row = block * STEP + n
            products(x_ref, pt_ref, column, jnp.minimum(row + 1, ROWS - 1), product_refs[(n + 1) % STEP])
            accumulate(pi_ref, place, row, product_refs[n], accs)

    def send(chunk):
        rows = pl.ds(pl.multiple_of(chunk * (CHUNK * 64), CHUNK * 64), CHUNK * 64)
        return pltpu.make_async_copy(out_ref.at[rows, :], out_hbm.at[rows, :], out_sems.at[chunk])

    @pl.loop(0, CHUNKS)
    def _(chunk):
        for g in range(CHUNK):
            finish(accs, fold_ref, out_ref, (chunk * CHUNK + g) * 4)
        send(chunk).start()

    @pl.loop(0, CHUNKS)
    def _(chunk):
        send(chunk).wait()


def combine(cols, slots, agg, x, left, own, right, other):
    vmem = pl.BlockSpec(memory_space=pltpu.VMEM)
    smem = pl.BlockSpec(memory_space=pltpu.SMEM)
    anywhere = pl.BlockSpec(memory_space=pl.ANY)
    return pl.pallas_call(
        kernel,
        out_shape=jax.ShapeDtypeStruct((AGGS * CSLOTS * 16, 128), F32),
        in_specs=[smem, smem, smem, vmem, vmem, vmem, vmem, vmem],
        out_specs=anywhere,
        scratch_shapes=[
            pltpu.VMEM((3 * ROWS, BLOCK, 128), BF16),
            pltpu.VMEM((ROWS, 2, BLOCK, 128), BF16),
            pltpu.VMEM((AGGS * CSLOTS, HALF, 128), F32),
            pltpu.VMEM((AGGS * CSLOTS, HALF, 128), F32),
            pltpu.VMEM((512, 1024), BF16),
            pltpu.VMEM((512, 2048), BF16),
            pltpu.VMEM((BLOCK, 256), BF16),
            pltpu.VMEM((AGGS * CSLOTS * 16, 128), F32),
            *[pltpu.VMEM((2, QUADS * HALF, 128), BF16)] * STEP,
            pltpu.SemaphoreType.DMA((CHUNKS,)),
        ],
        compiler_params=pltpu.CompilerParams(vmem_limit_bytes=36 << 20),
        name="galerkin",
    )(cols, slots, agg, x, left, own, right, other)


def shards(blocks, panels, columns, aggregate, coarse_slots):
    own = panels.reshape(ROWS, 2048)
    x, left, right, other = exchange(jnp.transpose(blocks, (1, 0, 2)), own)
    out = combine(columns.T, coarse_slots.T, aggregate, x, left, own, right, other)
    return out.reshape(AGGS, CSLOTS, 1, 2048)


def solution(mesh):
    return jax.shard_map(
        shards,
        mesh=mesh,
        in_specs=(
            P(("rows", "owners"), None, None),
            P(("rows", "owners"), "rep", None),
            P(("rows", "owners"), None),
            P(("rows", "owners")),
            P(("rows", "owners"), None),
        ),
        out_specs=P(("rows", "owners"), None, "rep", None),
        check_vma=False,
    )
```

```python
import jax
import jax.numpy as jnp
from jax import lax
from jax.experimental import pallas as pl
from jax.experimental.pallas import tpu as pltpu
from jax.sharding import PartitionSpec as P

BLOCK = 64
HALF = 32
SLOTS = 27
ROWS = 48
AGGS = 16
CSLOTS = 33
TILE = 16
TILES = ROWS // TILE
PART = 9
EARLY = 9
STEP = 16
FINE = 6144
QUADS = 7
CHUNK = 33
CHUNKS = AGGS * CSLOTS // 4 // CHUNK
F32 = jnp.float32
BF16 = jnp.bfloat16
NT = (((1,), (1,)), ((), ()))


def iota(shape, dim):
    return lax.broadcasted_iota(jnp.int32, shape, dim)


def one_hot(mask):
    return jnp.where(mask, 1.0, 0.0).astype(F32).astype(BF16)


def prepare(refs, rep, spread_ref, order_ref, pt_ref, pi_ref):
    def table(ref, width, shift, place_of):
        row, lane = iota((128, 8 * width), 0), iota((128, 8 * width), 1)
        ahead = place_of(lane & (width - 1)) - ((row >> 3) << 2)
        ahead = jnp.where((row & 7) == (lane >> shift), ahead, -1)
        for r in range(4):
            ref[r * 128:(r + 1) * 128, :] = one_hot(ahead == r)

    table(spread_ref, 128, 7, lambda p: p & 63)
    table(order_ref, 256, 8, lambda p: (((p >> 4) & 1) << 5) + ((p & 15) << 1) + (p >> 7))

    left, own, right, other = refs

    def transposed(ref):
        parts = []
        for q in range(TILES):
            rows16 = ref[q * TILE:(q + 1) * TILE, :].astype(F32)
            for half in range(2):
                rows8 = rows16[half * 8:half * 8 + 8, :]
                stacked = jnp.concatenate([rows8[:, u * 128:(u + 1) * 128] for u in range(16)], axis=0)
                turned = stacked.T.astype(BF16)
                parts.append(jnp.concatenate([turned[r * 32:(r + 1) * 32, :] for r in range(4)], axis=1))
        return jnp.concatenate(parts, axis=0)

    def put(result, width, store):
        result = result.astype(BF16)
        for group in range(6):
            for j in range(8):
                store(group * 8 + j, result[group * 32:(group + 1) * 32, j * width:(j + 1) * width])

    first = iota((HALF, 128), 1) < 64
    for base, ref in ((0, left), (ROWS, own), (2 * ROWS, right)):
        lhs = transposed(ref)

        def store_pt(j, value, base=base):
            zero = jnp.zeros_like(value)
            pt_ref[base + j, 0:HALF, :] = jnp.where(first, value, zero)
            pt_ref[base + j, HALF:BLOCK, :] = jnp.where(first, zero, value)

        put(jnp.dot(lhs, spread_ref[...], preferred_element_type=F32), 128, store_pt)
    for ref, half in ((own, rep), (other, 1 - rep)):
        lhs = transposed(ref)
        start = pl.multiple_of(half * HALF, HALF)

        def store_pi(i, value, start=start):
            pi_ref[i, 0, pl.ds(start, HALF), :] = value[:, 0:128]
            pi_ref[i, 1, pl.ds(start, HALF), :] = value[:, 128:256]

        put(jnp.dot(lhs, order_ref[...], preferred_element_type=F32), 256, store_pi)


def relayout(blocks_ref, x_ref, perm_ref, tile, k):
    native = blocks_ref[k, pl.ds(pl.multiple_of(tile * TILE, TILE), TILE), :]
    halves = []
    for high in range(2):
        halves.append(jnp.concatenate(
            [native[:, (high * 16 + t) * 128:(high * 16 + t + 1) * 128] for t in range(16)], axis=0))
    rhs = jnp.concatenate(halves, axis=1)
    result = jnp.dot(perm_ref[...], rhs, preferred_element_type=F32).astype(BF16)
    for i in range(TILE):
        x_ref[tile * TILE + i, k, 0:16, :] = result[i * 16:(i + 1) * 16, 0:128]
        x_ref[tile * TILE + i, k, 16:32, :] = result[i * 16:(i + 1) * 16, 128:256]


def products(x_ref, pt_ref, column, row, product_ref):
    zero = jnp.zeros((HALF, 128), BF16)

    def pair(k0, k1):
        lhs = jnp.concatenate([pt_ref[column(k0, row)], pt_ref[column(k1, row)]], axis=1)
        weights = jnp.concatenate([
            jnp.concatenate([x_ref[row, k0], zero], axis=1),
            jnp.concatenate([zero, x_ref[row, k1]], axis=1)], axis=0)
        return lax.dot_general(lhs, weights, NT, preferred_element_type=F32).astype(BF16)

    for group in range(QUADS):
        k = [min(group * 4 + n, SLOTS - 1) for n in range(4)]
        if k[2] < k[3]:
            last = pair(k[2], k[3])
        else:
            alone = lax.dot_general(pt_ref[column(k[2], row)], x_ref[row, k[2]], NT, preferred_element_type=F32)
            last = jnp.concatenate([alone.astype(BF16), jnp.zeros((BLOCK, HALF), BF16)], axis=1)
        both = jnp.concatenate([pair(k[0], k[1]), last], axis=1)
        rows = slice(group * HALF, (group + 1) * HALF)
        product_ref[0, rows, :] = both[0:HALF]
        product_ref[1, rows, :] = both[HALF:BLOCK]


def accumulate(pi_ref, place, row, product_ref, accs):
    block = iota((BLOCK, 128), 1) // 32
    even, odd = pi_ref[row, 0], pi_ref[row, 1]
    zero = jnp.zeros_like(even)
    weights = jnp.concatenate([
        jnp.concatenate([jnp.where(block == n, even, zero), jnp.where(block == n, odd, zero)], axis=1)
        for n in range(4)], axis=0)
    lhs = jnp.concatenate([product_ref[0], product_ref[1]], axis=1)
    triple = lax.dot_general(lhs, weights, NT, preferred_element_type=F32)
    for k in range(SLOTS):
        group, n = divmod(k, 4)
        at = place(k, row)
        lanes = slice((n % 2) * BLOCK, (n % 2 + 1) * BLOCK)
        value = triple[group * HALF:(group + 1) * HALF, n * BLOCK:(n + 1) * BLOCK]
        acc_ref = accs[n % 2]
        acc_ref[at, :, lanes] = acc_ref[at, :, lanes] + value


def finish(accs, fold_ref, out_ref, tile):
    side = iota((HALF, 128), 1) < BLOCK
    stacked = jnp.concatenate([jnp.where(side, accs[0][tile + s], accs[1][tile + s]) for s in range(4)], axis=0)
    head = stacked.astype(BF16)
    tail = (stacked - head.astype(F32)).astype(BF16)
    turned = lax.dot_general(
        fold_ref[...], jnp.concatenate([head, tail], axis=1), NT, preferred_element_type=F32)
    p = [turned[r * 16:(r + 1) * 16] for r in range(4)]
    lane = iota((16, 128), 1)
    low, even = lane < 64, lane % 64 < 32
    u = [jnp.where(low, p[0], pltpu.roll(p[2], 64, 1)), jnp.where(low, p[1], pltpu.roll(p[3], 64, 1)),
         jnp.where(low, pltpu.roll(p[0], 64, 1), p[2]), jnp.where(low, pltpu.roll(p[1], 64, 1), p[3])]
    for s in range(4):
        a, b = u[s // 2 * 2], u[s // 2 * 2 + 1]
        value = jnp.where(even, a, pltpu.roll(b, 32, 1)) if s % 2 == 0 else jnp.where(even, pltpu.roll(a, 96, 1), b)
        out_ref[pl.ds(pl.multiple_of((tile + s) * 16, 16), 16), :] = value


def exchange_kernel(blocks_hbm, own_hbm, x_ref, left_hbm, right_hbm, other_hbm,
                    blocks_ref, perm_ref, in_sems, send_sems, recv_sems):
    r, o, c = lax.axis_index("rows"), lax.axis_index("owners"), lax.axis_index("rep")
    rows, owners = lax.axis_size("rows"), lax.axis_size("owners")
    groups = rows * owners
    group = r * owners + o
    after, before = (group + 1) % groups, (group + groups - 1) % groups
    targets = [(after // owners, after % owners, c), (before // owners, before % owners, c), (r, o, 1 - c)]
    barrier = pltpu.get_barrier_semaphore()
    for target in targets:
        pl.semaphore_signal(barrier, inc=1, device_id=target, device_id_type=pl.DeviceIdType.MESH)

    def pieces(part):
        return pl.ds(pl.multiple_of(part // 3 * TILE, TILE), TILE), pl.ds(part % 3 * PART, PART)

    def fetch(part):
        rows_at, slots_at = pieces(part)
        return pltpu.make_async_copy(
            blocks_hbm.at[slots_at, rows_at, :], blocks_ref.at[slots_at, rows_at, :], in_sems.at[part])

    for part in range(EARLY):
        fetch(part).start()

    def turn(part, _):
        fetch(part).wait()
        for q in range(PART):
            relayout(blocks_ref, x_ref, perm_ref, part // 3, part % 3 * PART + q)
        return 0

    pl.semaphore_wait(barrier, 3)
    copies = []
    for n, (target, landing) in enumerate(zip(targets, (left_hbm, right_hbm, other_hbm))):
        copies.append(pltpu.make_async_remote_copy(
            src_ref=own_hbm, dst_ref=landing, send_sem=send_sems.at[n], recv_sem=recv_sems.at[n],
            device_id=target, device_id_type=pl.DeviceIdType.MESH))
    for copy in copies:
        copy.start()
    for part in range(EARLY, 9):
        fetch(part).start()
    row, lane = iota((256, 256), 0), iota((256, 256), 1)
    perm_ref[...] = one_hot((row // 16 == lane % 16) & (row % 16 == lane // 16))
    lax.fori_loop(0, 9, turn, 0)
    for copy in copies:
        copy.wait()


def exchange(blocks, own):
    anywhere = pl.BlockSpec(memory_space=pl.ANY)
    panel = pltpu.VMEM((ROWS, 2048), BF16)
    return pl.pallas_call(
        exchange_kernel,
        out_shape=(pltpu.VMEM((ROWS, SLOTS, HALF, 128), BF16), panel, panel, panel),
        in_specs=[anywhere, anywhere],
        out_specs=(pl.BlockSpec(memory_space=pltpu.VMEM),) * 4,
        scratch_shapes=[
            pltpu.VMEM((SLOTS, ROWS, BLOCK * BLOCK), BF16),
            pltpu.VMEM((256, 256), BF16),
            pltpu.SemaphoreType.DMA((9,)),
            pltpu.SemaphoreType.DMA((3,)),
            pltpu.SemaphoreType.DMA((3,)),
        ],
        compiler_params=pltpu.CompilerParams(
            vmem_limit_bytes=48 << 20, collective_id=0, has_side_effects=True),
        name="turn_blocks",
    )(blocks, own)


def kernel(cols_ref, slots_ref, agg_ref, x_ref, left_ref, own_ref, right_ref, other_ref, out_hbm,
           pt_ref, pi_ref, acc_ref, second_ref, spread_ref, order_ref, fold_ref, out_ref,
           *rest):
    product_refs, (out_sems,) = rest[:STEP], rest[STEP:]
    accs = (acc_ref, second_ref)
    group = lax.axis_index("rows") * lax.axis_size("owners") + lax.axis_index("owners")
    first_row, first_coarse = group * ROWS, group * AGGS

    prepare((left_ref, own_ref, right_ref, other_ref), lax.axis_index("rep"), spread_ref, order_ref, pt_ref, pi_ref)
    row, lane = iota((BLOCK, 256), 0), iota((BLOCK, 256), 1)
    fold_ref[...] = one_hot(4 * (row % 16) + row // 16 == lane % 64)

    @pl.loop(0, AGGS)
    def _(t):
        for s in range(CSLOTS):
            acc_ref[t * CSLOTS + s, :, 0:BLOCK] = jnp.zeros((HALF, BLOCK), F32)
            second_ref[t * CSLOTS + s, :, BLOCK:128] = jnp.zeros((HALF, BLOCK), F32)

    def column(k, row):
        near = cols_ref[k, row] - first_row + ROWS
        near = jnp.where(near < 0, near + FINE, near)
        return jnp.where(near >= FINE, near - FINE, near)

    def place(k, row):
        return (agg_ref[row] - first_coarse) * CSLOTS + slots_ref[k, row]

    products(x_ref, pt_ref, column, 0, product_refs[0])

    @pl.loop(0, ROWS // STEP)
    def _(block):
        for n in range(STEP):
            row = block * STEP + n
            products(x_ref, pt_ref, column, jnp.minimum(row + 1, ROWS - 1), product_refs[(n + 1) % STEP])
            accumulate(pi_ref, place, row, product_refs[n], accs)

    def send(chunk):
        rows = pl.ds(pl.multiple_of(chunk * (CHUNK * 64), CHUNK * 64), CHUNK * 64)
        return pltpu.make_async_copy(out_ref.at[rows, :], out_hbm.at[rows, :], out_sems.at[chunk])

    @pl.loop(0, CHUNKS)
    def _(chunk):
        for g in range(CHUNK):
            finish(accs, fold_ref, out_ref, (chunk * CHUNK + g) * 4)
        send(chunk).start()

    @pl.loop(0, CHUNKS)
    def _(chunk):
        send(chunk).wait()


def combine(cols, slots, agg, x, left, own, right, other):
    vmem = pl.BlockSpec(memory_space=pltpu.VMEM)
    smem = pl.BlockSpec(memory_space=pltpu.SMEM)
    anywhere = pl.BlockSpec(memory_space=pl.ANY)
    return pl.pallas_call(
        kernel,
        out_shape=jax.ShapeDtypeStruct((AGGS * CSLOTS * 16, 128), F32),
        in_specs=[smem, smem, smem, vmem, vmem, vmem, vmem, vmem],
        out_specs=anywhere,
        scratch_shapes=[
            pltpu.VMEM((3 * ROWS, BLOCK, 128), BF16),
            pltpu.VMEM((ROWS, 2, BLOCK, 128), BF16),
            pltpu.VMEM((AGGS * CSLOTS, HALF, 128), F32),
            pltpu.VMEM((AGGS * CSLOTS, HALF, 128), F32),
            pltpu.VMEM((512, 1024), BF16),
            pltpu.VMEM((512, 2048), BF16),
            pltpu.VMEM((BLOCK, 256), BF16),
            pltpu.VMEM((AGGS * CSLOTS * 16, 128), F32),
            *[pltpu.VMEM((2, QUADS * HALF, 128), BF16)] * STEP,
            pltpu.SemaphoreType.DMA((CHUNKS,)),
        ],
        compiler_params=pltpu.CompilerParams(vmem_limit_bytes=36 << 20),
        name="galerkin",
    )(cols, slots, agg, x, left, own, right, other)


def shards(blocks, panels, columns, aggregate, coarse_slots):
    own = panels.reshape(ROWS, 2048)
    x, left, right, other = exchange(jnp.transpose(blocks, (1, 0, 2)), own)
    out = combine(columns.T, coarse_slots.T, aggregate, x, left, own, right, other)
    return out.reshape(AGGS, CSLOTS, 1, 2048)


def solution(mesh):
    return jax.shard_map(
        shards,
        mesh=mesh,
        in_specs=(
            P(("rows", "owners"), None, None),
            P(("rows", "owners"), "rep", None),
            P(("rows", "owners"), None),
            P(("rows", "owners")),
            P(("rows", "owners"), None),
        ),
        out_specs=P(("rows", "owners"), None, "rep", None),
        check_vma=False,
    )
```
